256 devices in a mesh: space: 32 (over z, y), member: 8 (over x, core).
Axes of the slice: x: 4, y: 4, z: 8, core: 2. Of those that a mesh axis runs over, the one named last changes fastest.
Arguments:
- increment: bfloat16 [3072, 64, 128], P('space', 'member'), may hold values from -6 to 6
- interp: bfloat16 [3072, 128, 128], P('space'), may hold values from -0.25 to 0.25
- owner: int32 [3072, 1], P('space'), may hold values from 0 to 31; in each aligned block of 96 rows (0 to 95, 96 to 191, ...) at most 6 rows name the same one
- local_block: int32 [3072], P('space'), may hold values from 0 to 23
- ensemble: bfloat16 [80, 768, 64, 128], P('member', 'space'), may hold values from -6 to 6
- modes: float32 [64, 4], replicated, may hold values from -2 to 2
Outputs:
- applied_fine: float32 [3072, 64, 128], P('space', 'member')
The draws below stay inside these ranges and needn't reach their ends.
Inputs may be any that keep to these rules, and one draw needn't show every extreme that they name: `owner`: among the rows of one device no value appears more than 6 times, and some value appears exactly 6 times.
All inputs are finite; a program needn't handle non-finite values.
Results may differ from the reference program's by a relative error of at most 0.0038.
Values may be sent and summed in bfloat16 or wider, within the bound.
A program may use at most 64 MiB of HBM per device.

```python
import math
import jax
import jax.numpy as jnp
import numpy as np
from jax import lax

LEV = 64
MODES = 4
BW = 128
CBD = 24
FINE_DEV = 96
CAP = 6
CBLOCKS = 768
FBLOCKS = 3072
MEMBERS = 80
N_SPACE = 32


def touch_ends(result, rng, low, high):
    dims = result.shape
    spot = [jax.random.randint(jax.random.fold_in(rng, axis), (), 0, dims[axis]) for axis in range(len(dims))]
    result = result.at[tuple(spot)].set(low)
    longest = dims.index(max(dims))
    spot[longest] = (spot[longest] + 1) % dims[longest]
    return result.at[tuple(spot)].set(high)


def block_levels(stream_key, dims, cuts, smallest, high):
    loudness, own = 1.0, jax.random.fold_in(stream_key, 6)
    for position, parts in cuts:
        draws = jnp.exp(jax.random.uniform(jax.random.fold_in(own, position), (parts,), jnp.float32, smallest / len(cuts), high / len(cuts)))
        loudness = loudness * jnp.repeat(draws, dims[position] // parts).reshape([-1 if axis == position else 1 for axis in range(len(dims))])
    return loudness


def deal_out(key, own, number, rows, count, top, bound, slope):
    order = jax.random.permutation(key, count)
    crowded, ordinary = load_shares(count, rows * top, bound, slope, True), load_shares(count, rows * top, bound, slope, False)
    places = jnp.arange(count)

    def named(lengths, turn):
        used = int((lengths > 0).sum())
        fixed = max(1, used // 4)
        shifted = fixed + (places - fixed + turn * (used - fixed)) % max(1, count - fixed)
        return jnp.zeros((count,), jnp.int32).at[order[jnp.where(places < fixed, places, shifted)]].set(jnp.asarray(lengths, jnp.int32))

    lengths = jnp.where(number % 4 == 0, named(crowded, number // 4), named(ordinary, number - number // 4 - 1))
    mixed = jax.random.permutation(jax.random.fold_in(own, 3), count)
    donor, sink = mixed[0:count // 2 * 2:2], mixed[1:count // 2 * 2:2]
    room = jnp.minimum(lengths[donor] - 1, bound - lengths[sink]) // 2
    room = jnp.where((donor == order[0]) | (sink == order[0]) | (lengths[sink] == 0), 0, jnp.maximum(room, 0))
    shifted = jax.random.randint(jax.random.fold_in(own, 4), (count // 2,), 0, 1 << 20) % (room + 1)
    lengths = lengths.at[donor].add(-shifted).at[sink].add(shifted)
    members = jnp.searchsorted(jnp.cumsum(lengths), jnp.arange(rows * top), side="right").astype(jnp.int32)
    listing = members.reshape(top, rows).T
    listing = listing[jax.random.permutation(jax.random.fold_in(own, 1), rows)]
    turn = jax.random.randint(jax.random.fold_in(own, 2), (rows, 1), 0, top)
    return jnp.take_along_axis(listing, (jnp.arange(top)[None, :] + turn) % top, axis=1)


def load_shares(amount, total, most, slope, full):
    weights = [(1 << 20) // math.isqrt(grade ** slope) + 1 for grade in range(1, amount + 1)]
    largest = most if full else min(most, max(-(-total // amount), total * weights[0] // sum(weights)))
    least = 1 if total - largest >= amount - 1 else 0
    counts, surplus = [largest] + [least] * (amount - 1), total - largest - least * (amount - 1)
    while surplus > 0:
        movable = [i for i in range(1, amount) if counts[i] < largest] or [i for i in range(1, amount) if counts[i] < most]
        pool, remaining = sum([weights[i] for i in movable]), surplus
        for i in movable:
            more = min(most - counts[i], max(1, remaining * weights[i] // pool), surplus)
            counts[i] = counts[i] + more
            surplus = surplus - more
    return np.array(counts)


def gaussian(rng, shape, width, reach, cuts=(), held_as=jnp.bfloat16):
    result = jax.random.normal(rng, shape, jnp.float32) * width
    if len(cuts) > 0:
        result = block_levels(rng, shape, cuts, -0.22, 0.18) * result
    return jnp.clip(result, min=-reach, max=reach).astype(held_as)


def setup_inputs(seed: int = 0) -> dict:
    key_list = jax.random.split(jax.random.key(seed), 7)
    increment = gaussian(key_list[0], (FBLOCKS, LEV, BW), 1.0, 6.0, ((0, 32), (1, 8)))
    interp = gaussian(key_list[1], (FBLOCKS, BW, BW), (4 * BW) ** -0.5, 0.25, ((0, 32),))
    owner_keys = jax.random.split(jax.random.fold_in(key_list[2], 1), FBLOCKS // FINE_DEV)
    owner_turns = jax.random.permutation(jax.random.fold_in(key_list[2], 3), FBLOCKS // FINE_DEV)
    owner = jax.vmap(lambda own, number: deal_out(jax.random.fold_in(key_list[2], 2), own, number, FINE_DEV, N_SPACE, 1, CAP, 2))(owner_keys, owner_turns).reshape((FBLOCKS, 1))
    local_block = touch_ends(jax.random.randint(key_list[3], (FBLOCKS,), 0, CBD), jax.random.fold_in(key_list[3], 1), 0, CBD - 1).astype(jnp.int32)
    ensemble = gaussian(key_list[4], (MEMBERS, CBLOCKS, LEV, BW), 1.0, 6.0, ((0, 8), (1, 32)))
    modes = gaussian(key_list[5], (LEV, MODES), 0.35, 2.0, (), jnp.float32)
    return {"increment": increment, "interp": interp, "owner": owner, "local_block": local_block, "ensemble": ensemble, "modes": modes}


def reference(increment, interp, owner, local_block, ensemble, modes):
    highest = lax.Precision.HIGHEST
    weights = interp.astype(jnp.float32)
    pieces = jnp.einsum("bli,bij->blj", increment.astype(jnp.float32), weights, precision=highest)
    target = (owner[:, 0] * CBD + local_block).astype(jnp.int32)
    restricted = jax.ops.segment_sum(pieces, target, num_segments=CBLOCKS).astype(jnp.bfloat16)
    restricted_wide = restricted.astype(jnp.float32)

    def member_step(total, member):
        values = member.astype(jnp.float32)
        schur = values * restricted_wide
        coefficients = jnp.einsum("clj,lk->ckj", schur, modes, precision=highest)
        rebuilt = jnp.einsum("ckj,lk->clj", coefficients, modes, precision=highest)
        return total + values * rebuilt, None

    start = jnp.zeros((CBLOCKS, LEV, BW), jnp.float32)
    total = lax.scan(member_step, start, ensemble)[0]
    applied = (total / (MEMBERS - 1)).astype(jnp.bfloat16)
    fine_values = applied[target].astype(jnp.float32)
    return jnp.einsum("blj,bij->bli", fine_values, weights, precision=highest)
```

```python
import functools
import jax
import jax.numpy as jnp
from jax import lax
from jax.experimental import pallas as pl
from jax.experimental.pallas import tpu as pltpu
from jax.sharding import PartitionSpec as P

MESH = pl.DeviceIdType.MESH
CAP = 6
F32 = jnp.float32
BF16 = jnp.bfloat16


def iota(shape, dim):
    return lax.broadcasted_iota(jnp.int32, shape, dim)


def dot(a, b):
    return jnp.dot(a, b, preferred_element_type=F32)


def one_hot(condition):
    return jnp.where(condition, 1.0, 0.0).astype(BF16)


def kernel(
    dims,
    interp_hbm,
    inc_hbm,
    ens_hbm,
    owner_ref,
    local_ref,
    modes_ref,
    out_ref,
    interp,
    inc,
    ens,
    pieces,
    send,
    recv,
    idx_send,
    idx_recv,
    unplace,
    collect,
    spread,
    levels_buf,
    contrib,
    arrived,
    reply,
    back,
    fine,
    load_sem,
    send_sem,
    recv_sem,
):
    n_space, n_member, fine_count, lev, members, coarse, width, chunks, scale = dims
    rows = CAP * lev
    slots = n_space * rows
    fine_rows = fine_count * lev
    coarse_rows = coarse * lev
    me = lax.axis_index("space")
    group = lax.axis_index("member")
    per = fine_count // chunks

    inc_copy = pltpu.make_async_copy(inc_hbm, inc, load_sem.at[chunks])
    inc_copy.start()
    loads = []
    for t in range(chunks):
        part = pl.ds(t * per, per)
        copy = pltpu.make_async_copy(interp_hbm.at[part], interp.at[part], load_sem.at[t])
        copy.start()
        loads.append(copy)
    ens_copy = pltpu.make_async_copy(ens_hbm, ens, load_sem.at[chunks + 1])
    ens_copy.start()

    barrier = pltpu.get_barrier_semaphore()

    def greet_space(k, carry):
        peer = {"space": lax.rem(me + k, n_space)}
        pl.semaphore_signal(barrier, inc=1, device_id=peer, device_id_type=MESH)
        return carry

    def greet_member(k, carry):
        peer = {"member": lax.rem(group + k, n_member)}
        pl.semaphore_signal(barrier, inc=1, device_id=peer, device_id_type=MESH)
        return carry

    lax.fori_loop(1, n_space, greet_space, 0)
    lax.fori_loop(1, n_member, greet_member, 0)

    owner_col = owner_ref[...].astype(F32)
    own_b = jnp.broadcast_to(owner_col, (fine_count, fine_count))
    down, across = iota((fine_count, fine_count), 0), iota((fine_count, fine_count), 1)
    owner_row = jnp.sum(jnp.where(down == across, own_b, 0.0), axis=0, keepdims=True)
    same = own_b == owner_row
    rank_row = jnp.sum(jnp.where(same & (down < across), 1.0, 0.0), axis=0, keepdims=True)
    rank_col = jnp.sum(jnp.where(same & (across < down), 1.0, 0.0), axis=1, keepdims=True)
    slot_row = owner_row * CAP + rank_row
    slot_col = owner_col * CAP + rank_col

    local_row = local_ref[...].astype(F32) + 1.0
    by_owner = jnp.where(
        iota((n_space, fine_count), 0).astype(F32) == owner_row, local_row, 0.0
    ).astype(BF16)
    by_rank = one_hot(iota((fine_count, 128), 1).astype(F32) == rank_col)
    table = dot(by_owner, by_rank)
    for d in range(n_space):
        idx_send[d] = table[d : d + 1, :]

    widen = one_hot(iota((fine_count, fine_rows), 1) // lev == iota((fine_count, fine_rows), 0))
    place_row = dot(jnp.broadcast_to(slot_row, (8, fine_count)).astype(BF16), widen)[0:1]
    place_row = place_row * lev + (iota((1, fine_rows), 1) % lev).astype(F32)

    inc_copy.wait()
    for t in range(chunks):
        loads[t].wait()

        @pl.loop(0, per // 2, unroll=4)
        def _(i):
            b = t * per + i * 2
            first = dot(inc[b], interp[b])
            second = dot(inc[b + 1], interp[b + 1])
            both = jnp.concatenate([first, second], axis=0).astype(BF16)
            pieces[pl.ds(pl.multiple_of(b * lev, 2 * lev), 2 * lev), :] = both

    pl.semaphore_wait(barrier, n_space - 1 + n_member - 1)

    def space_copy(src, dst, d, phase):
        return pltpu.make_async_remote_copy(
            src_ref=src,
            dst_ref=dst,
            send_sem=send_sem.at[phase],
            recv_sem=recv_sem.at[phase],
            device_id={"space": d},
            device_id_type=MESH,
        )

    def member_copy(src, dst, d, phase):
        return pltpu.make_async_remote_copy(
            src_ref=src,
            dst_ref=dst,
            send_sem=send_sem.at[phase],
            recv_sem=recv_sem.at[phase],
            device_id={"member": d},
            device_id_type=MESH,
        )

    def send_idx(k, carry):
        d = lax.rem(me + k, n_space)
        space_copy(idx_send.at[d], idx_recv.at[me], d, 0).start()
        return carry

    lax.fori_loop(1, n_space, send_idx, 0)

    per_step = 4
    step_rows = per_step * rows
    packed = pieces[...]

    def place(k, carry):
        first = lax.rem((me // per_step + k) * per_step, n_space)
        row = iota((step_rows, fine_rows), 0).astype(F32)
        wanted = place_row - (first * rows).astype(F32)
        values = dot(one_hot(row == wanted), packed).astype(BF16)
        for q in range(per_step):
            d = first + q
            send[d] = values[q * rows : (q + 1) * rows, :]

            @pl.when(d != me)
            def _():
                space_copy(send.at[d], recv.at[me], d, 1).start()

        return carry

    lax.fori_loop(1, n_space // per_step + 1, place, 0)
    recv[me] = send[me]
    idx_recv[me] = idx_send[me]

    widen_col = one_hot(iota((fine_rows, fine_count), 0) // lev == iota((fine_rows, fine_count), 1))
    slot_wide = jnp.broadcast_to(slot_col, (fine_count, 128)).astype(BF16)
    place_col = dot(widen_col, slot_wide) * lev + (iota((fine_rows, 128), 0) % lev).astype(F32)
    for t in range(slots // 128):
        unplace[:, t * 128 : (t + 1) * 128] = one_hot(
            place_col == (iota((fine_rows, 128), 1) + t * 128).astype(F32)
        )

    idx_all = space_copy(
        idx_send.at[pl.ds(0, n_space - 1)],
        idx_recv.at[pl.ds(0, n_space - 1)],
        lax.rem(me + 1, n_space),
        0,
    )
    idx_all.wait_recv()
    index = jnp.concatenate([idx_recv[s] for s in range(n_space)], axis=0).astype(BF16)
    lane_rank = one_hot((iota((128, slots), 1) % rows) // lev == iota((128, slots), 0))
    by_source = dot(index, lane_rank)
    mine = iota((n_space, slots), 1) // rows == iota((n_space, slots), 0)
    index_row = jnp.sum(jnp.where(mine, by_source, 0.0), axis=0, keepdims=True)
    index_row = (index_row - 1.0) * lev + (iota((1, slots), 1) % lev).astype(F32)
    collect[...] = one_hot(iota((coarse_rows, slots), 0).astype(F32) == index_row)
    source_of = one_hot(iota((slots, n_space), 0) // rows == iota((slots, n_space), 1))
    by_row = dot(source_of, index)
    rank_of = (iota((slots, 128), 0) % rows) // lev == iota((slots, 128), 1)
    index_col = jnp.sum(jnp.where(rank_of, by_row, 0.0), axis=1, keepdims=True)
    index_col = (index_col - 1.0) * lev + (iota((slots, 1), 0) % lev).astype(F32)
    spread[...] = one_hot(iota((slots, coarse_rows), 1).astype(F32) == index_col)

    mix = lax.dot_general(
        modes_ref[...],
        modes_ref[...],
        (((1,), (1,)), ((), ())),
        precision=lax.Precision.HIGHEST,
        preferred_element_type=F32,
    )
    mix_high = mix.astype(BF16)
    mix_low = (mix - mix_high.astype(F32)).astype(BF16)
    mix_both = jnp.concatenate([mix_high, mix_low], axis=1)

    space_copy(
        send.at[pl.ds(0, n_space - 1)],
        recv.at[pl.ds(0, n_space - 1)],
        lax.rem(me + 1, n_space),
        1,
    ).wait_recv()
    restricted = dot(collect[...], recv[...].reshape(slots, width)).astype(BF16)
    levels_buf[group] = restricted

    def send_levels(k, carry):
        d = lax.rem(group + k, n_member)
        member_copy(levels_buf.at[group], levels_buf.at[group], d, 2).start()
        return carry

    lax.fori_loop(1, n_member, send_levels, 0)
    ens_copy.wait()
    member_copy(
        levels_buf.at[pl.ds(0, n_member - 1)],
        levels_buf.at[pl.ds(0, n_member - 1)],
        lax.rem(group + 1, n_member),
        2,
    ).wait_recv()

    def coarse_pair(i, carry):
        at = pl.multiple_of(i * 2 * lev, 2 * lev)
        slabs = [levels_buf[g, pl.ds(at, 2 * lev), :].astype(F32) for g in range(n_member)]
        totals = []
        for half in range(2):
            c = i * 2 + half
            here = jnp.concatenate(
                [slab[half * lev : (half + 1) * lev] for slab in slabs], axis=0
            ).astype(BF16)
            schur = jnp.concatenate([ens[m, c] * here for m in range(members)], axis=1)
            rebuilt = dot(mix_both, jnp.concatenate([schur, schur], axis=0))
            total = jnp.zeros(here.shape, F32)
            for m in range(members):
                total += ens[m, c].astype(F32) * rebuilt[:, m * width : (m + 1) * width]
            totals.append(total)
        for g in range(n_member):
            contrib[g, pl.ds(at, 2 * lev), :] = jnp.concatenate(
                [total[g * lev : (g + 1) * lev] for total in totals], axis=0
            ).astype(BF16)
        return carry

    lax.fori_loop(0, coarse // 2, coarse_pair, 0)

    def send_contrib(k, carry):
        d = lax.rem(group + k, n_member)
        member_copy(contrib.at[d], arrived.at[group], d, 3).start()
        return carry

    lax.fori_loop(1, n_member, send_contrib, 0)
    arrived[group] = contrib[group]
    member_copy(
        contrib.at[pl.ds(0, n_member - 1)],
        arrived.at[pl.ds(0, n_member - 1)],
        lax.rem(group + 1, n_member),
        3,
    ).wait_recv()
    applied = arrived[0].astype(F32)
    for g in range(1, n_member):
        applied += arrived[g].astype(F32)
    applied = (applied / scale).astype(BF16)

    def answer(k, carry):
        first = lax.rem((me // per_step + k) * per_step, n_space)
        at = pl.multiple_of(first * rows, step_rows)
        values = dot(spread[pl.ds(at, step_rows), :], applied).astype(BF16)
        for q in range(per_step):
            d = first + q
            reply[d] = values[q * rows : (q + 1) * rows, :]

            @pl.when(d != me)
            def _():
                space_copy(reply.at[d], back.at[me], d, 4).start()

        return carry

    lax.fori_loop(1, n_space // per_step + 1, answer, 0)
    back[me] = reply[me]
    space_copy(
        reply.at[pl.ds(0, n_space - 1)],
        back.at[pl.ds(0, n_space - 1)],
        lax.rem(me + 1, n_space),
        4,
    ).wait_recv()
    fine[...] = dot(unplace[...], back[...].reshape(slots, width)).astype(BF16)

    @pl.loop(0, fine_count // 2, unroll=4)
    def _(i):
        b = i * 2
        both = fine[pl.ds(pl.multiple_of(b * lev, 2 * lev), 2 * lev), :]
        for half in range(2):
            out_ref[b + half] = lax.dot_general(
                both[half * lev : (half + 1) * lev],
                interp[b + half],
                (((1,), (1,)), ((), ())),
                preferred_element_type=F32,
            )

    def sent(src, d, make, phase):
        make(src, src, d, phase).wait_send()

    other = lax.rem(me + 1, n_space)
    sent(idx_send.at[pl.ds(0, n_space - 1)], other, space_copy, 0)
    sent(send.at[pl.ds(0, n_space - 1)], other, space_copy, 1)
    sent(levels_buf.at[pl.ds(0, n_member - 1)], lax.rem(group + 1, n_member), member_copy, 2)
    sent(contrib.at[pl.ds(0, n_member - 1)], lax.rem(group + 1, n_member), member_copy, 3)
    sent(reply.at[pl.ds(0, n_space - 1)], other, space_copy, 4)


def on_device(increment, interp, owner, local_block, ensemble, modes):
    fine_count, lev, width = increment.shape
    members, coarse, all_lev, _ = ensemble.shape
    n_space, n_member = lax.axis_size("space"), lax.axis_size("member")
    chunks = 6
    scale = float(members * n_member - 1)
    dims = (n_space, n_member, fine_count, lev, members, coarse, width, chunks, scale)
    rows = CAP * lev
    slots = n_space * rows
    anywhere = pl.BlockSpec(memory_space=pl.ANY)
    vmem = pl.BlockSpec(memory_space=pltpu.VMEM)
    exchange = pltpu.VMEM((n_space, rows, width), BF16)
    by_group = pltpu.VMEM((n_member, coarse * lev, width), BF16)
    return pl.pallas_call(
        functools.partial(kernel, dims),
        out_shape=jax.ShapeDtypeStruct((fine_count, lev, width), F32),
        in_specs=[anywhere, anywhere, anywhere, vmem, vmem, vmem],
        out_specs=vmem,
        scratch_shapes=[
            pltpu.VMEM(interp.shape, BF16),
            pltpu.VMEM(increment.shape, BF16),
            pltpu.VMEM(ensemble.shape, BF16),
            pltpu.VMEM((fine_count * lev, width), BF16),
            exchange,
            exchange,
            pltpu.VMEM((n_space, 1, 128), F32),
            pltpu.VMEM((n_space, 1, 128), F32),
            pltpu.VMEM((fine_count * lev, slots), BF16),
            pltpu.VMEM((coarse * lev, slots), BF16),
            pltpu.VMEM((slots, coarse * lev), BF16),
            by_group,
            by_group,
            by_group,
            exchange,
            exchange,
            pltpu.VMEM((fine_count * lev, width), BF16),
            pltpu.SemaphoreType.DMA((chunks + 2,)),
            pltpu.SemaphoreType.DMA((5,)),
            pltpu.SemaphoreType.DMA((5,)),
        ],
        compiler_params=pltpu.CompilerParams(
            collective_id=0, has_side_effects=True, vmem_limit_bytes=48 * 1024 * 1024
        ),
        name="covariance_apply",
    )(interp, increment, ensemble, owner, local_block.reshape(1, fine_count), modes)


def solution(mesh):
    in_specs = (
        P("space", "member", None),
        P("space", None, None),
        P("space", None),
        P("space"),
        P("member", "space", None, None),
        P(),
    )
    out_specs = P("space", "member", None)
    return jax.shard_map(
        on_device, mesh=mesh, in_specs=in_specs, out_specs=out_specs, check_vma=False
    )
```

```python
import functools
import jax
import jax.numpy as jnp
from jax import lax
from jax.experimental import pallas as pl
from jax.experimental.pallas import tpu as pltpu
from jax.sharding import PartitionSpec as P

MESH = pl.DeviceIdType.MESH
CAP = 6
F32 = jnp.float32
BF16 = jnp.bfloat16


def iota(shape, dim):
    return lax.broadcasted_iota(jnp.int32, shape, dim)


def dot(a, b):
    return jnp.dot(a, b, preferred_element_type=F32)


def one_hot(condition):
    return jnp.where(condition, 1.0, 0.0).astype(BF16)


def kernel(
    dims,
    interp_hbm,
    inc_hbm,
    ens_hbm,
    owner_hbm,
    local_hbm,
    modes_hbm,
    out_ref,
    owner_ref,
    local_ref,
    modes_ref,
    interp,
    inc,
    ens,
    pieces,
    send,
    recv,
    idx_send,
    idx_recv,
    unplace,
    collect,
    spread,
    levels_buf,
    contrib,
    arrived,
    reply,
    back,
    fine,
    load_sem,
    send_sem,
    recv_sem,
):
    n_space, n_member, fine_count, lev, members, coarse, width, chunks, parts, n_y, scale = dims
    rows = CAP * lev
    slots = n_space * rows
    fine_rows = fine_count * lev
    coarse_rows = coarse * lev
    me = lax.axis_index("space")
    group = lax.axis_index("member")
    per = fine_count // chunks

    def load(src, dst, i):
        copy = pltpu.make_async_copy(src, dst, load_sem.at[i])
        copy.start()
        return copy

    owner_copy = load(owner_hbm, owner_ref, chunks + 2)
    local_copy = load(local_hbm, local_ref, chunks + 3)
    inc_copy = load(inc_hbm, inc, chunks)
    loads = []
    for t in range(chunks):
        part = pl.ds(t * per, per)
        loads.append(load(interp_hbm.at[part], interp.at[part], t))
    modes_copy = load(modes_hbm, modes_ref, chunks + 4)

    last = n_space - 1
    n_z = n_space // n_y
    my_z, my_y = me // n_y, lax.rem(me, n_y)

    def peer_at(p):
        k = last - p
        k_y, k_z = k // n_z, lax.rem(k, n_z)
        half = (k_z + 1) // 2
        up = lax.rem(k_z, 2) == 1
        step_z = jnp.where(up, half, n_z - half)
        device = lax.rem(my_z + step_z, n_z) * n_y + lax.rem(my_y + k_y, n_y)
        paired = (k_z == 0) | (k_z == n_z - 1)
        back_z = jnp.where(paired, k_z, jnp.where(up, k_z + 1, k_z - 1))
        return device, last - (lax.rem(n_y - k_y, n_y) * n_z + back_z)

    def position_of(device):
        step_z = (device // n_y - my_z + n_z) % n_z
        step_y = (device % n_y - my_y + n_y) % n_y
        k_z = jnp.where(
            step_z <= n_z // 2, jnp.maximum(2 * step_z - 1, 0), 2 * (n_z - step_z)
        )
        return last - (step_y * n_z + k_z)

    barrier = pltpu.get_barrier_semaphore()

    def greet_space(k, carry):
        peer = {"space": lax.rem(me + k, n_space)}
        pl.semaphore_signal(barrier, inc=1, device_id=peer, device_id_type=MESH)
        return carry

    def greet_member(k, carry):
        peer = {"member": lax.rem(group + k, n_member)}
        pl.semaphore_signal(barrier, inc=1, device_id=peer, device_id_type=MESH)
        return carry

    lax.fori_loop(1, n_space, greet_space, 0)
    lax.fori_loop(1, n_member, greet_member, 0)

    owner_copy.wait()
    local_copy.wait()
    owner_row = position_of(owner_ref[...]).astype(F32)
    down, across = iota((fine_count, fine_count), 0), iota((fine_count, fine_count), 1)
    owner_col = jnp.sum(jnp.where(down == across, owner_row, 0.0), axis=1, keepdims=True)
    same = owner_col == owner_row
    rank_row = jnp.sum(jnp.where(same & (down < across), 1.0, 0.0), axis=0, keepdims=True)
    rank_col = jnp.sum(jnp.where(same & (across < down), 1.0, 0.0), axis=1, keepdims=True)
    slot_row = owner_row * CAP + rank_row
    slot_col = owner_col * CAP + rank_col

    local_row = local_ref[...].astype(F32) + 1.0
    by_owner = jnp.where(
        iota((n_space, fine_count), 0).astype(F32) == owner_row, local_row, 0.0
    ).astype(BF16)
    by_rank = one_hot(iota((fine_count, 128), 1).astype(F32) == rank_col)
    table = dot(by_owner, by_rank)
    for d in range(n_space):
        idx_send[d] = table[d : d + 1, :]

    widen = one_hot(iota((fine_count, fine_rows), 1) // lev == iota((fine_count, fine_rows), 0))
    place_row = dot(jnp.broadcast_to(slot_row, (8, fine_count)).astype(BF16), widen)[0:1]
    place_row = place_row * lev + (iota((1, fine_rows), 1) % lev).astype(F32)

    inc_copy.wait()
    for t in range(chunks):
        loads[t].wait()

        @pl.loop(0, per // 2, unroll=4)
        def _(i):
            b = t * per + i * 2
            first = dot(inc[b], interp[b])
            second = dot(inc[b + 1], interp[b + 1])
            both = jnp.concatenate([first, second], axis=0).astype(BF16)
            pieces[pl.ds(pl.multiple_of(b * lev, 2 * lev), 2 * lev), :] = both

    ens_copy = load(ens_hbm, ens, chunks + 1)
    pl.semaphore_wait(barrier, n_space - 1 + n_member - 1)

    def space_copy(src, dst, d, phase):
        return pltpu.make_async_remote_copy(
            src_ref=src,
            dst_ref=dst,
            send_sem=send_sem.at[phase],
            recv_sem=recv_sem.at[phase],
            device_id={"space": d},
            device_id_type=MESH,
        )

    def member_copy(src, dst, d, phase):
        return pltpu.make_async_remote_copy(
            src_ref=src,
            dst_ref=dst,
            send_sem=send_sem.at[phase],
            recv_sem=recv_sem.at[phase],
            device_id={"member": d},
            device_id_type=MESH,
        )

    def send_idx(k, carry):
        d, there = peer_at(k)
        space_copy(idx_send.at[k], idx_recv.at[there], d, 0).start()
        return carry

    lax.fori_loop(0, last, send_idx, 0)

    per_step = 4
    step_rows = per_step * rows
    packed = pieces[...]

    def place(k, carry):
        row = iota((step_rows, fine_rows), 0).astype(F32)
        wanted = place_row - (k * step_rows).astype(F32)
        values = dot(one_hot(row == wanted), packed).astype(BF16)
        for q in range(per_step):
            p = k * per_step + q
            send[p] = values[q * rows : (q + 1) * rows, :]

            @pl.when(p != last)
            def _():
                d, there = peer_at(p)
                space_copy(send.at[p], recv.at[there], d, 1).start()

        return carry

    lax.fori_loop(0, n_space // per_step, place, 0)
    recv[last] = send[last]
    idx_recv[last] = idx_send[last]

    widen_col = one_hot(iota((fine_rows, fine_count), 0) // lev == iota((fine_rows, fine_count), 1))
    slot_wide = jnp.broadcast_to(slot_col, (fine_count, 128)).astype(BF16)
    place_col = dot(widen_col, slot_wide) * lev + (iota((fine_rows, 128), 0) % lev).astype(F32)
    for t in range(slots // 128):
        unplace[:, t * 128 : (t + 1) * 128] = one_hot(
            place_col == (iota((fine_rows, 128), 1) + t * 128).astype(F32)
        )

    idx_all = space_copy(
        idx_send.at[pl.ds(0, n_space - 1)],
        idx_recv.at[pl.ds(0, n_space - 1)],
        lax.rem(me + 1, n_space),
        0,
    )
    idx_all.wait_recv()
    index = jnp.concatenate([idx_recv[s] for s in range(n_space)], axis=0).astype(BF16)
    lane_rank = one_hot((iota((128, slots), 1) % rows) // lev == iota((128, slots), 0))
    by_source = dot(index, lane_rank)
    mine = iota((n_space, slots), 1) // rows == iota((n_space, slots), 0)
    index_row = jnp.sum(jnp.where(mine, by_source, 0.0), axis=0, keepdims=True)
    index_row = (index_row - 1.0) * lev + (iota((1, slots), 1) % lev).astype(F32)
    collect[...] = one_hot(iota((coarse_rows, slots), 0).astype(F32) == index_row)
    source_of = one_hot(iota((slots, n_space), 0) // rows == iota((slots, n_space), 1))
    by_row = dot(source_of, index)
    rank_of = (iota((slots, 128), 0) % rows) // lev == iota((slots, 128), 1)
    index_col = jnp.sum(jnp.where(rank_of, by_row, 0.0), axis=1, keepdims=True)
    index_col = (index_col - 1.0) * lev + (iota((slots, 1), 0) % lev).astype(F32)
    spread[...] = one_hot(iota((slots, coarse_rows), 1).astype(F32) == index_col)

    modes_copy.wait()
    mix = lax.dot_general(
        modes_ref[...],
        modes_ref[...],
        (((0,), (0,)), ((), ())),
        precision=lax.Precision.HIGHEST,
        preferred_element_type=F32,
    )
    mix_high = mix.astype(BF16)
    mix_low = (mix - mix_high.astype(F32)).astype(BF16)
    mix_both = jnp.concatenate([mix_high, mix_low], axis=1)

    space_copy(
        send.at[pl.ds(0, n_space - 1)],
        recv.at[pl.ds(0, n_space - 1)],
        lax.rem(me + 1, n_space),
        1,
    ).wait_recv()
    restricted = dot(collect[...], recv[...].reshape(slots, width)).astype(BF16)
    part_rows = coarse_rows // parts
    for q in range(parts):
        levels_buf[q, group] = restricted[q * part_rows : (q + 1) * part_rows]

        def send_levels(k, carry):
            d = lax.rem(group + k, n_member)
            member_copy(levels_buf.at[q, group], levels_buf.at[q, group], d, 2 + q).start()
            return carry

        lax.fori_loop(1, n_member, send_levels, 0)
    ens_copy.wait()

    others = pl.ds(0, n_member - 1)
    next_member = lax.rem(group + 1, n_member)
    for q in range(parts):
        member_copy(
            levels_buf.at[q, others], levels_buf.at[q, others], next_member, 2 + q
        ).wait_recv()

        def coarse_pair(i, carry):
            at = pl.multiple_of(i * 2 * lev, 2 * lev)
            slabs = [
                levels_buf[q, g, pl.ds(at, 2 * lev), :].astype(F32) for g in range(n_member)
            ]
            totals = []
            for half in range(2):
                c = q * (coarse // parts) + i * 2 + half
                here = jnp.concatenate(
                    [slab[half * lev : (half + 1) * lev] for slab in slabs], axis=0
                ).astype(BF16)
                schur = jnp.concatenate([ens[m, c] * here for m in range(members)], axis=1)
                rebuilt = dot(mix_both, jnp.concatenate([schur, schur], axis=0))
                total = jnp.zeros(here.shape, F32)
                for m in range(members):
                    total += ens[m, c].astype(F32) * rebuilt[:, m * width : (m + 1) * width]
                totals.append(total)
            for g in range(n_member):
                contrib[q, g, pl.ds(at, 2 * lev), :] = jnp.concatenate(
                    [total[g * lev : (g + 1) * lev] for total in totals], axis=0
                ).astype(BF16)
            return carry

        lax.fori_loop(0, coarse // parts // 2, coarse_pair, 0)

        def send_contrib(k, carry):
            d = lax.rem(group + k, n_member)
            member_copy(
                contrib.at[q, d], arrived.at[q, group], d, 2 + parts + q
            ).start()
            return carry

        lax.fori_loop(1, n_member, send_contrib, 0)
        arrived[q, group] = contrib[q, group]

    summed = []
    for q in range(parts):
        member_copy(
            contrib.at[q, others], arrived.at[q, others], next_member, 2 + parts + q
        ).wait_recv()
        total = arrived[q, 0].astype(F32)
        for g in range(1, n_member):
            total += arrived[q, g].astype(F32)
        summed.append((total / scale).astype(BF16))
    applied = jnp.concatenate(summed, axis=0)

    def answer(k, carry):
        at = pl.multiple_of(k * step_rows, step_rows)
        values = dot(spread[pl.ds(at, step_rows), :], applied).astype(BF16)
        for q in range(per_step):
            p = k * per_step + q
            reply[p] = values[q * rows : (q + 1) * rows, :]

            @pl.when(p != last)
            def _():
                d, there = peer_at(p)
                space_copy(reply.at[p], back.at[there], d, 2 + 2 * parts).start()

        return carry

    lax.fori_loop(0, n_space // per_step, answer, 0)
    back[last] = reply[last]
    space_copy(
        reply.at[pl.ds(0, n_space - 1)],
        back.at[pl.ds(0, n_space - 1)],
        lax.rem(me + 1, n_space),
        2 + 2 * parts,
    ).wait_recv()
    fine[...] = dot(unplace[...], back[...].reshape(slots, width)).astype(BF16)

    @pl.loop(0, fine_count // 2, unroll=4)
    def _(i):
        b = i * 2
        both = fine[pl.ds(pl.multiple_of(b * lev, 2 * lev), 2 * lev), :]
        for half in range(2):
            out_ref[b + half] = lax.dot_general(
                both[half * lev : (half + 1) * lev],
                interp[b + half],
                (((1,), (1,)), ((), ())),
                preferred_element_type=F32,
            )

    def sent(src, d, make, phase):
        make(src, src, d, phase).wait_send()

    other = lax.rem(me + 1, n_space)
    sent(idx_send.at[pl.ds(0, n_space - 1)], other, space_copy, 0)
    sent(send.at[pl.ds(0, n_space - 1)], other, space_copy, 1)
    for q in range(parts):
        sent(levels_buf.at[q, others], next_member, member_copy, 2 + q)
        sent(contrib.at[q, others], next_member, member_copy, 2 + parts + q)
    sent(reply.at[pl.ds(0, n_space - 1)], other, space_copy, 2 + 2 * parts)


def on_device(increment, interp, owner, local_block, ensemble, modes):
    fine_count, lev, width = increment.shape
    members, coarse, all_lev, _ = ensemble.shape
    n_space, n_member = lax.axis_size("space"), lax.axis_size("member")
    chunks = 6
    scale = float(members * n_member - 1)
    parts, n_y = 4, 4
    dims = (
        n_space, n_member, fine_count, lev, members, coarse, width, chunks, parts, n_y, scale
    )
    rows = CAP * lev
    slots = n_space * rows
    arguments = (
        interp,
        increment,
        ensemble,
        owner.reshape(1, fine_count),
        local_block.reshape(1, fine_count),
        modes.T,
    )
    hbm = pl.BlockSpec(memory_space=pltpu.HBM)
    vmem = pl.BlockSpec(memory_space=pltpu.VMEM)
    exchange = pltpu.VMEM((n_space, rows, width), BF16)
    by_group = pltpu.VMEM((parts, n_member, coarse // parts * lev, width), BF16)
    return pl.pallas_call(
        functools.partial(kernel, dims),
        out_shape=jax.ShapeDtypeStruct((fine_count, lev, width), F32),
        in_specs=[hbm] * 6,
        out_specs=vmem,
        scratch_shapes=[
            pltpu.VMEM((1, fine_count), jnp.int32),
            pltpu.VMEM((1, fine_count), jnp.int32),
            pltpu.VMEM(modes.shape[::-1], F32),
            pltpu.VMEM(interp.shape, BF16),
            pltpu.VMEM(increment.shape, BF16),
            pltpu.VMEM(ensemble.shape, BF16),
            pltpu.VMEM((fine_count * lev, width), BF16),
            exchange,
            exchange,
            pltpu.VMEM((n_space, 1, 128), F32),
            pltpu.VMEM((n_space, 1, 128), F32),
            pltpu.VMEM((fine_count * lev, slots), BF16),
            pltpu.VMEM((coarse * lev, slots), BF16),
            pltpu.VMEM((slots, coarse * lev), BF16),
            by_group,
            by_group,
            by_group,
            exchange,
            exchange,
            pltpu.VMEM((fine_count * lev, width), BF16),
            pltpu.SemaphoreType.DMA((chunks + 5,)),
            pltpu.SemaphoreType.DMA((3 + 2 * parts,)),
            pltpu.SemaphoreType.DMA((3 + 2 * parts,)),
        ],
        compiler_params=pltpu.CompilerParams(
            collective_id=0, has_side_effects=True, vmem_limit_bytes=48 * 1024 * 1024
        ),
        name="covariance_apply",
    )(*[pltpu.with_memory_space_constraint(a, pltpu.HBM) for a in arguments])


def solution(mesh):
    in_specs = (
        P("space", "member", None),
        P("space", None, None),
        P("space", None),
        P("space"),
        P("member", "space", None, None),
        P(),
    )
    out_specs = P("space", "member", None)
    return jax.shard_map(
        on_device, mesh=mesh, in_specs=in_specs, out_specs=out_specs, check_vma=False
    )
```

```python
import functools
import jax
import jax.numpy as jnp
from jax import lax
from jax.experimental import pallas as pl
from jax.experimental.pallas import tpu as pltpu
from jax.sharding import PartitionSpec as P

MESH = pl.DeviceIdType.MESH
CAP = 6
F32 = jnp.float32
BF16 = jnp.bfloat16


def iota(shape, dim):
    return lax.broadcasted_iota(jnp.int32, shape, dim)


def dot(a, b):
    return jnp.dot(a, b, preferred_element_type=F32)


def one_hot(condition):
    return jnp.where(condition, 1.0, 0.0).astype(BF16)


def kernel(
    dims,
    interp_hbm,
    inc_hbm,
    ens_hbm,
    owner_hbm,
    local_hbm,
    modes_hbm,
    out_ref,
    owner_ref,
    local_ref,
    modes_ref,
    interp,
    inc,
    ens,
    pieces,
    send,
    recv,
    idx_send,
    idx_recv,
    placing,
    unplace,
    collect,
    spread,
    levels_buf,
    contrib,
    arrived,
    reply,
    back,
    fine,
    load_sem,
    send_sem,
    recv_sem,
):
    n_space, n_member, fine_count, lev, members, coarse, width, chunks, parts, n_y, scale = dims
    rows = CAP * lev
    slots = n_space * rows
    fine_rows = fine_count * lev
    coarse_rows = coarse * lev
    me = lax.axis_index("space")
    group = lax.axis_index("member")
    per = fine_count // chunks

    barrier = pltpu.get_barrier_semaphore()

    def greet_space(k, carry):
        peer = {"space": lax.rem(me + k, n_space)}
        pl.semaphore_signal(barrier, inc=1, device_id=peer, device_id_type=MESH)
        return carry

    def greet_member(k, carry):
        peer = {"member": lax.rem(group + k, n_member)}
        pl.semaphore_signal(barrier, inc=1, device_id=peer, device_id_type=MESH)
        return carry

    lax.fori_loop(1, n_space, greet_space, 0)
    lax.fori_loop(1, n_member, greet_member, 0)

    def load(src, dst, i):
        copy = pltpu.make_async_copy(src, dst, load_sem.at[i])
        copy.start()
        return copy

    owner_copy = load(owner_hbm, owner_ref, chunks + 2)
    local_copy = load(local_hbm, local_ref, chunks + 3)
    inc_copy = load(inc_hbm, inc, chunks)
    loads = []
    for t in range(chunks):
        part = pl.ds(t * per, per)
        loads.append(load(interp_hbm.at[part], interp.at[part], t))
    modes_copy = load(modes_hbm, modes_ref, chunks + 4)

    def member_at(k):
        third = lax.rem(k, 3)
        step = jnp.where(third == 0, 2, jnp.where(third == 1, 1, 3))
        step = jnp.where(k == n_member - 2, 0, step)
        core = lax.rem(group, 2)
        flip = (k < 3) | (k == n_member - 2)
        return lax.rem(group // 2 + step, n_member // 2) * 2 + jnp.where(flip, 1 - core, core)

    last = n_space - 1
    n_z = n_space // n_y
    my_z, my_y = me // n_y, lax.rem(me, n_y)

    def peer_at(p):
        k = last - p
        k_y, k_z = k // n_z, lax.rem(k, n_z)
        half = (k_z + 1) // 2
        up = lax.rem(k_z, 2) == 1
        step_z = jnp.where(up, half, n_z - half)
        device = lax.rem(my_z + step_z, n_z) * n_y + lax.rem(my_y + k_y, n_y)
        paired = (k_z == 0) | (k_z == n_z - 1)
        back_z = jnp.where(paired, k_z, jnp.where(up, k_z + 1, k_z - 1))
        return device, last - (lax.rem(n_y - k_y, n_y) * n_z + back_z)

    def position_of(device):
        step_z = (device // n_y - my_z + n_z) % n_z
        step_y = (device % n_y - my_y + n_y) % n_y
        k_z = jnp.where(
            step_z <= n_z // 2, jnp.maximum(2 * step_z - 1, 0), 2 * (n_z - step_z)
        )
        return last - (step_y * n_z + k_z)

    owner_copy.wait()
    local_copy.wait()
    owner_row = position_of(owner_ref[...]).astype(F32)
    down, across = iota((fine_count, fine_count), 0), iota((fine_count, fine_count), 1)
    owner_col = jnp.sum(jnp.where(down == across, owner_row, 0.0), axis=1, keepdims=True)
    same = owner_col == owner_row
    rank_row = jnp.sum(jnp.where(same & (down < across), 1.0, 0.0), axis=0, keepdims=True)
    rank_col = jnp.sum(jnp.where(same & (across < down), 1.0, 0.0), axis=1, keepdims=True)
    slot_row = owner_row * CAP + rank_row
    slot_col = owner_col * CAP + rank_col

    local_row = local_ref[...].astype(F32) + 1.0
    by_owner = jnp.where(
        iota((n_space, fine_count), 0).astype(F32) == owner_row, local_row, 0.0
    ).astype(BF16)
    by_rank = one_hot(iota((fine_count, 128), 1).astype(F32) == rank_col)
    table = dot(by_owner, by_rank)
    for d in range(n_space):
        idx_send[d] = table[d : d + 1, :]

    widen = one_hot(iota((fine_count, fine_rows), 1) // lev == iota((fine_count, fine_rows), 0))
    place_row = dot(jnp.broadcast_to(slot_row, (8, fine_count)).astype(BF16), widen)[0:1]
    place_row = place_row * lev + (iota((1, fine_rows), 1) % lev).astype(F32)

    per_step = 4
    step_rows = per_step * rows
    for k in range(n_space // per_step):
        row = (iota((step_rows, fine_rows), 0) + k * step_rows).astype(F32)
        placing[k * step_rows : (k + 1) * step_rows, :] = one_hot(row == place_row)

    inc_copy.wait()
    for t in range(chunks):
        loads[t].wait()

        @pl.loop(0, per // 2, unroll=4)
        def _(i):
            b = t * per + i * 2
            first = dot(inc[b], interp[b])
            second = dot(inc[b + 1], interp[b + 1])
            both = jnp.concatenate([first, second], axis=0).astype(BF16)
            pieces[pl.ds(pl.multiple_of(b * lev, 2 * lev), 2 * lev), :] = both

    ens_copy = load(ens_hbm, ens, chunks + 1)
    pl.semaphore_wait(barrier, n_space - 1 + n_member - 1)

    def space_copy(src, dst, d, phase):
        return pltpu.make_async_remote_copy(
            src_ref=src,
            dst_ref=dst,
            send_sem=send_sem.at[phase],
            recv_sem=recv_sem.at[phase],
            device_id={"space": d},
            device_id_type=MESH,
        )

    def member_copy(src, dst, d, phase):
        return pltpu.make_async_remote_copy(
            src_ref=src,
            dst_ref=dst,
            send_sem=send_sem.at[phase],
            recv_sem=recv_sem.at[phase],
            device_id={"member": d},
            device_id_type=MESH,
        )

    def send_idx(k, carry):
        d, there = peer_at(k)
        space_copy(idx_send.at[k], idx_recv.at[there], d, 0).start()
        return carry

    lax.fori_loop(0, last, send_idx, 0)

    packed = pieces[...]

    def place(k, carry):
        at = pl.multiple_of(k * step_rows, step_rows)
        values = dot(placing[pl.ds(at, step_rows), :], packed).astype(BF16)
        for q in range(per_step):
            p = k * per_step + q
            send[p] = values[q * rows : (q + 1) * rows, :]

            @pl.when(p != last)
            def _():
                d, there = peer_at(p)
                space_copy(send.at[p], recv.at[there], d, 1).start()

        return carry

    lax.fori_loop(0, n_space // per_step, place, 0)
    recv[last] = send[last]
    idx_recv[last] = idx_send[last]

    idx_all = space_copy(
        idx_send.at[pl.ds(0, n_space - 1)],
        idx_recv.at[pl.ds(0, n_space - 1)],
        lax.rem(me + 1, n_space),
        0,
    )
    idx_all.wait_recv()
    index = jnp.concatenate([idx_recv[s] for s in range(n_space)], axis=0).astype(BF16)
    lane_rank = one_hot((iota((128, slots), 1) % rows) // lev == iota((128, slots), 0))
    by_source = dot(index, lane_rank)
    mine = iota((n_space, slots), 1) // rows == iota((n_space, slots), 0)
    index_row = jnp.sum(jnp.where(mine, by_source, 0.0), axis=0, keepdims=True)
    index_row = (index_row - 1.0) * lev + (iota((1, slots), 1) % lev).astype(F32)
    collect[...] = one_hot(iota((coarse_rows, slots), 0).astype(F32) == index_row)
    source_of = one_hot(iota((slots, n_space), 0) // rows == iota((slots, n_space), 1))
    by_row = dot(source_of, index)
    rank_of = (iota((slots, 128), 0) % rows) // lev == iota((slots, 128), 1)
    index_col = jnp.sum(jnp.where(rank_of, by_row, 0.0), axis=1, keepdims=True)
    index_col = (index_col - 1.0) * lev + (iota((slots, 1), 0) % lev).astype(F32)
    spread[...] = one_hot(iota((slots, coarse_rows), 1).astype(F32) == index_col)

    modes_copy.wait()
    mix = lax.dot_general(
        modes_ref[...],
        modes_ref[...],
        (((0,), (0,)), ((), ())),
        precision=lax.Precision.HIGHEST,
        preferred_element_type=F32,
    )
    mix_high = mix.astype(BF16)
    mix_low = (mix - mix_high.astype(F32)).astype(BF16)
    mix_both = jnp.concatenate([mix_high, mix_low], axis=1)

    space_copy(
        send.at[pl.ds(0, n_space - 1)],
        recv.at[pl.ds(0, n_space - 1)],
        lax.rem(me + 1, n_space),
        1,
    ).wait_recv()
    restricted = dot(collect[...], recv[...].reshape(slots, width)).astype(BF16)
    part_rows = coarse_rows // parts
    for q in range(parts):
        levels_buf[q, group] = restricted[q * part_rows : (q + 1) * part_rows]

        def send_levels(k, carry):
            d = member_at(k)
            member_copy(levels_buf.at[q, group], levels_buf.at[q, group], d, 2 + q).start()
            return carry

        lax.fori_loop(0, n_member - 1, send_levels, 0)
    @pl.loop(0, fine_count, unroll=4)
    def _(b):
        interp[b] = interp[b].T

    widen_col = one_hot(iota((fine_rows, fine_count), 0) // lev == iota((fine_rows, fine_count), 1))
    slot_wide = jnp.broadcast_to(slot_col, (fine_count, 128)).astype(BF16)
    place_col = dot(widen_col, slot_wide) * lev + (iota((fine_rows, 128), 0) % lev).astype(F32)
    for t in range(slots // 128):
        unplace[:, t * 128 : (t + 1) * 128] = one_hot(
            place_col == (iota((fine_rows, 128), 1) + t * 128).astype(F32)
        )

    ens_copy.wait()

    others = pl.ds(0, n_member - 1)
    next_member = lax.rem(group + 1, n_member)
    for q in range(parts):
        member_copy(
            levels_buf.at[q, others], levels_buf.at[q, others], next_member, 2 + q
        ).wait_recv()

        def coarse_pair(i, carry):
            at = pl.multiple_of(i * 2 * lev, 2 * lev)
            slabs = [
                levels_buf[q, g, pl.ds(at, 2 * lev), :].astype(F32) for g in range(n_member)
            ]
            totals = []
            for half in range(2):
                c = q * (coarse // parts) + i * 2 + half
                here = jnp.concatenate(
                    [slab[half * lev : (half + 1) * lev] for slab in slabs], axis=0
                ).astype(BF16)
                schur = jnp.concatenate([ens[m, c] * here for m in range(members)], axis=1)
                rebuilt = dot(mix_both, jnp.concatenate([schur, schur], axis=0))
                total = jnp.zeros(here.shape, F32)
                for m in range(members):
                    total += ens[m, c].astype(F32) * rebuilt[:, m * width : (m + 1) * width]
                totals.append(total)
            for g in range(n_member):
                contrib[q, g, pl.ds(at, 2 * lev), :] = jnp.concatenate(
                    [total[g * lev : (g + 1) * lev] for total in totals], axis=0
                ).astype(BF16)
            return carry

        lax.fori_loop(0, coarse // parts // 2, coarse_pair, 0)

        def send_contrib(k, carry):
            d = member_at(k)
            member_copy(
                contrib.at[q, d], arrived.at[q, group], d, 2 + parts + q
            ).start()
            return carry

        lax.fori_loop(0, n_member - 1, send_contrib, 0)
        arrived[q, group] = contrib[q, group]

    summed = []
    for q in range(parts):
        member_copy(
            contrib.at[q, others], arrived.at[q, others], next_member, 2 + parts + q
        ).wait_recv()
        total = arrived[q, 0].astype(F32)
        for g in range(1, n_member):
            total += arrived[q, g].astype(F32)
        summed.append((total / scale).astype(BF16))
    applied = jnp.concatenate(summed, axis=0)

    def answer(k, carry):
        at = pl.multiple_of(k * step_rows, step_rows)
        values = dot(spread[pl.ds(at, step_rows), :], applied).astype(BF16)
        for q in range(per_step):
            p = k * per_step + q
            reply[p] = values[q * rows : (q + 1) * rows, :]

            @pl.when(p != last)
            def _():
                d, there = peer_at(p)
                space_copy(reply.at[p], back.at[there], d, 2 + 2 * parts).start()

        return carry

    lax.fori_loop(0, n_space // per_step, answer, 0)
    back[last] = reply[last]
    space_copy(
        reply.at[pl.ds(0, n_space - 1)],
        back.at[pl.ds(0, n_space - 1)],
        lax.rem(me + 1, n_space),
        2 + 2 * parts,
    ).wait_recv()
    fine[...] = dot(unplace[...], back[...].reshape(slots, width)).astype(BF16)

    @pl.loop(0, fine_count // 2, unroll=4)
    def _(i):
        b = i * 2
        both = fine[pl.ds(pl.multiple_of(b * lev, 2 * lev), 2 * lev), :]
        for half in range(2):
            out_ref[b + half] = lax.dot_general(
                both[half * lev : (half + 1) * lev],
                interp[b + half],
                (((1,), (0,)), ((), ())),
                preferred_element_type=F32,
            )

    def sent(src, d, make, phase):
        make(src, src, d, phase).wait_send()

    other = lax.rem(me + 1, n_space)
    sent(idx_send.at[pl.ds(0, n_space - 1)], other, space_copy, 0)
    sent(send.at[pl.ds(0, n_space - 1)], other, space_copy, 1)
    for q in range(parts):
        sent(levels_buf.at[q, others], next_member, member_copy, 2 + q)
        sent(contrib.at[q, others], next_member, member_copy, 2 + parts + q)
    sent(reply.at[pl.ds(0, n_space - 1)], other, space_copy, 2 + 2 * parts)


def on_device(increment, interp, owner, local_block, ensemble, modes):
    fine_count, lev, width = increment.shape
    members, coarse, all_lev, _ = ensemble.shape
    n_space, n_member = lax.axis_size("space"), lax.axis_size("member")
    chunks = 6
    scale = float(members * n_member - 1)
    parts, n_y = 4, 4
    dims = (
        n_space, n_member, fine_count, lev, members, coarse, width, chunks, parts, n_y, scale
    )
    rows = CAP * lev
    slots = n_space * rows
    arguments = (
        interp,
        increment,
        ensemble,
        owner.reshape(1, fine_count),
        local_block.reshape(1, fine_count),
        modes.T,
    )
    hbm = pl.BlockSpec(memory_space=pltpu.HBM)
    vmem = pl.BlockSpec(memory_space=pltpu.VMEM)
    exchange = pltpu.VMEM((n_space, rows, width), BF16)
    by_group = pltpu.VMEM((parts, n_member, coarse // parts * lev, width), BF16)
    return pl.pallas_call(
        functools.partial(kernel, dims),
        out_shape=jax.ShapeDtypeStruct((fine_count, lev, width), F32),
        in_specs=[hbm] * 6,
        out_specs=vmem,
        scratch_shapes=[
            pltpu.VMEM((1, fine_count), jnp.int32),
            pltpu.VMEM((1, fine_count), jnp.int32),
            pltpu.VMEM(modes.shape[::-1], F32),
            pltpu.VMEM(interp.shape, BF16),
            pltpu.VMEM(increment.shape, BF16),
            pltpu.VMEM(ensemble.shape, BF16),
            pltpu.VMEM((fine_count * lev, width), BF16),
            exchange,
            exchange,
            pltpu.VMEM((n_space, 1, 128), F32),
            pltpu.VMEM((n_space, 1, 128), F32),
            pltpu.VMEM((slots, fine_count * lev), BF16),
            pltpu.VMEM((fine_count * lev, slots), BF16),
            pltpu.VMEM((coarse * lev, slots), BF16),
            pltpu.VMEM((slots, coarse * lev), BF16),
            by_group,
            by_group,
            by_group,
            exchange,
            exchange,
            pltpu.VMEM((fine_count * lev, width), BF16),
            pltpu.SemaphoreType.DMA((chunks + 5,)),
            pltpu.SemaphoreType.DMA((3 + 2 * parts,)),
            pltpu.SemaphoreType.DMA((3 + 2 * parts,)),
        ],
        compiler_params=pltpu.CompilerParams(
            collective_id=0, has_side_effects=True, vmem_limit_bytes=48 * 1024 * 1024
        ),
        name="covariance_apply",
    )(*[pltpu.with_memory_space_constraint(a, pltpu.HBM) for a in arguments])


def solution(mesh):
    in_specs = (
        P("space", "member", None),
        P("space", None, None),
        P("space", None),
        P("space"),
        P("member", "space", None, None),
        P(),
    )
    out_specs = P("space", "member", None)
    return jax.shard_map(
        on_device, mesh=mesh, in_specs=in_specs, out_specs=out_specs, check_vma=False
    )
```

```python
import functools
import jax
import jax.numpy as jnp
from jax import lax
from jax.experimental import pallas as pl
from jax.experimental.pallas import tpu as pltpu
from jax.sharding import PartitionSpec as P

MESH = pl.DeviceIdType.MESH
CAP = 6
F32 = jnp.float32
BF16 = jnp.bfloat16


def iota(shape, dim):
    return lax.broadcasted_iota(jnp.int32, shape, dim)


def dot(a, b):
    return jnp.dot(a, b, preferred_element_type=F32)


def one_hot(condition):
    return jnp.where(condition, 1.0, 0.0).astype(BF16)


def kernel(
    dims,
    interp_hbm,
    inc_hbm,
    ens_hbm,
    owner_hbm,
    local_hbm,
    modes_hbm,
    out_ref,
    owner_ref,
    local_ref,
    modes_ref,
    interp,
    inc,
    ens,
    pairs,
    pieces,
    send,
    recv,
    idx_send,
    idx_recv,
    placing,
    unplace,
    collect,
    spread,
    levels_buf,
    contrib,
    arrived,
    reply,
    back,
    fine,
    load_sem,
    send_sem,
    recv_sem,
):
    n_space, n_member, fine_count, lev, members, coarse, width, chunks, parts, n_y, scale = dims
    near = lev // 2
    wide = width // 2
    rows = CAP * near
    slots = n_space * rows
    fine_rows = fine_count * near
    coarse_rows = coarse * near
    me = lax.axis_index("space")
    group = lax.axis_index("member")
    per = fine_count // chunks

    barrier = pltpu.get_barrier_semaphore()

    def greet_space(k, carry):
        peer = {"space": lax.rem(me + k, n_space)}
        pl.semaphore_signal(barrier, inc=1, device_id=peer, device_id_type=MESH)
        return carry

    def greet_member(k, carry):
        peer = {"member": lax.rem(group + k, n_member)}
        pl.semaphore_signal(barrier, inc=1, device_id=peer, device_id_type=MESH)
        return carry

    lax.fori_loop(1, n_space, greet_space, 0)
    lax.fori_loop(1, n_member, greet_member, 0)

    def load(src, dst, i):
        copy = pltpu.make_async_copy(src, dst, load_sem.at[i])
        copy.start()
        return copy

    owner_copy = load(owner_hbm, owner_ref, chunks + 2)
    local_copy = load(local_hbm, local_ref, chunks + 3)
    inc_copy = load(inc_hbm, inc, chunks)
    loads = []
    for t in range(chunks):
        part = pl.ds(t * per, per)
        loads.append(load(interp_hbm.at[part], interp.at[part], t))
    modes_copy = load(modes_hbm, modes_ref, chunks + 4)

    def member_at(k):
        third = lax.rem(k, 3)
        step = jnp.where(third == 0, 2, jnp.where(third == 1, 1, 3))
        step = jnp.where(k == n_member - 2, 0, step)
        core = lax.rem(group, 2)
        flip = (k < 3) | (k == n_member - 2)
        return lax.rem(group // 2 + step, n_member // 2) * 2 + jnp.where(flip, 1 - core, core)

    last = n_space - 1
    n_z = n_space // n_y
    my_z, my_y = me // n_y, lax.rem(me, n_y)

    def peer_at(p):
        k = last - p
        k_y, k_z = k // n_z, lax.rem(k, n_z)
        half = (k_z + 1) // 2
        up = lax.rem(k_z, 2) == 1
        step_z = jnp.where(up, half, n_z - half)
        device = lax.rem(my_z + step_z, n_z) * n_y + lax.rem(my_y + k_y, n_y)
        paired = (k_z == 0) | (k_z == n_z - 1)
        back_z = jnp.where(paired, k_z, jnp.where(up, k_z + 1, k_z - 1))
        return device, last - (lax.rem(n_y - k_y, n_y) * n_z + back_z)

    def position_of(device):
        step_z = (device // n_y - my_z + n_z) % n_z
        step_y = (device % n_y - my_y + n_y) % n_y
        k_z = jnp.where(
            step_z <= n_z // 2, jnp.maximum(2 * step_z - 1, 0), 2 * (n_z - step_z)
        )
        return last - (step_y * n_z + k_z)

    owner_copy.wait()
    local_copy.wait()
    owner_row = position_of(owner_ref[...]).astype(F32)
    down, across = iota((fine_count, fine_count), 0), iota((fine_count, fine_count), 1)
    owner_col = jnp.sum(jnp.where(down == across, owner_row, 0.0), axis=1, keepdims=True)
    same = owner_col == owner_row
    rank_row = jnp.sum(jnp.where(same & (down < across), 1.0, 0.0), axis=0, keepdims=True)
    rank_col = jnp.sum(jnp.where(same & (across < down), 1.0, 0.0), axis=1, keepdims=True)
    slot_row = owner_row * CAP + rank_row
    slot_col = owner_col * CAP + rank_col

    local_row = local_ref[...].astype(F32) + 1.0
    by_owner = jnp.where(
        iota((n_space, fine_count), 0).astype(F32) == owner_row, local_row, 0.0
    ).astype(BF16)
    by_rank = one_hot(iota((fine_count, 128), 1).astype(F32) == rank_col)
    table = dot(by_owner, by_rank)
    for d in range(n_space):
        idx_send[d] = table[d : d + 1, :]

    widen = one_hot(iota((fine_count, fine_rows), 1) // near == iota((fine_count, fine_rows), 0))
    place_row = dot(jnp.broadcast_to(slot_row, (8, fine_count)).astype(BF16), widen)[0:1]
    place_row = place_row * near + (iota((1, fine_rows), 1) % near).astype(F32)

    per_step = 8
    step_rows = per_step * rows
    for k in range(n_space // per_step):
        row = (iota((step_rows, fine_rows), 0) + k * step_rows).astype(F32)
        placing[k * step_rows : (k + 1) * step_rows, :] = one_hot(row == place_row)

    low = iota((4 * near, width), 1) < wide

    def turned(x):
        return pltpu.roll(x, wide, 1)

    inc_copy.wait()
    for t in range(chunks):
        loads[t].wait()

        @pl.loop(0, per // 4, unroll=2)
        def _(i):
            b = t * per + i * 4
            four = [dot(inc[b + q], interp[b + q]) for q in range(4)]
            first = jnp.concatenate([v[:near] for v in four], axis=0)
            second = jnp.concatenate([v[near:] for v in four], axis=0)
            at = pl.ds(pl.multiple_of(b * near, 4 * near), 4 * near)
            pieces[0, at, :] = jnp.where(low, first, turned(second)).astype(BF16)
            pieces[1, at, :] = jnp.where(low, turned(first), second).astype(BF16)

    ens_copy = load(ens_hbm, ens, chunks + 1)
    pl.semaphore_wait(barrier, n_space - 1 + n_member - 1)

    def space_copy(src, dst, d, phase):
        return pltpu.make_async_remote_copy(
            src_ref=src,
            dst_ref=dst,
            send_sem=send_sem.at[phase],
            recv_sem=recv_sem.at[phase],
            device_id={"space": d},
            device_id_type=MESH,
        )

    def member_copy(src, dst, d, phase):
        return pltpu.make_async_remote_copy(
            src_ref=src,
            dst_ref=dst,
            send_sem=send_sem.at[phase],
            recv_sem=recv_sem.at[phase],
            device_id={"member": d},
            device_id_type=MESH,
        )

    def send_idx(k, carry):
        d, there = peer_at(k)
        space_copy(idx_send.at[k], idx_recv.at[there], d, 0).start()
        return carry

    lax.fori_loop(0, last, send_idx, 0)

    for h in range(2):
        packed = pieces[h]

        def place(k, carry):
            at = pl.multiple_of(k * step_rows, step_rows)
            values = dot(placing[pl.ds(at, step_rows), :], packed)
            for q in range(per_step):
                p = k * per_step + q
                send[h, p] = values[q * rows : (q + 1) * rows, :].astype(BF16)

                @pl.when(p != last)
                def _():
                    d, there = peer_at(p)
                    space_copy(send.at[h, p], recv.at[h, there], d, 1 + h).start()

            return carry

        lax.fori_loop(0, n_space // per_step, place, 0)
        recv[h, last] = send[h, last]
    idx_recv[last] = idx_send[last]

    idx_all = space_copy(
        idx_send.at[pl.ds(0, n_space - 1)],
        idx_recv.at[pl.ds(0, n_space - 1)],
        lax.rem(me + 1, n_space),
        0,
    )
    idx_all.wait_recv()
    index = jnp.concatenate([idx_recv[s] for s in range(n_space)], axis=0).astype(BF16)
    lane_rank = one_hot((iota((128, slots), 1) % rows) // near == iota((128, slots), 0))
    by_source = dot(index, lane_rank)
    mine = iota((n_space, slots), 1) // rows == iota((n_space, slots), 0)
    index_row = jnp.sum(jnp.where(mine, by_source, 0.0), axis=0, keepdims=True)
    index_row = (index_row - 1.0) * near + (iota((1, slots), 1) % near).astype(F32)
    collect[...] = one_hot(iota((coarse_rows, slots), 0).astype(F32) == index_row)
    source_of = one_hot(iota((slots, n_space), 0) // rows == iota((slots, n_space), 1))
    by_row = dot(source_of, index)
    rank_of = (iota((slots, 128), 0) % rows) // near == iota((slots, 128), 1)
    index_col = jnp.sum(jnp.where(rank_of, by_row, 0.0), axis=1, keepdims=True)
    index_col = (index_col - 1.0) * near + (iota((slots, 1), 0) % near).astype(F32)
    spread[...] = one_hot(iota((slots, coarse_rows), 1).astype(F32) == index_col)

    modes_copy.wait()
    mix = lax.dot_general(
        modes_ref[...],
        modes_ref[...],
        (((0,), (0,)), ((), ())),
        precision=lax.Precision.HIGHEST,
        preferred_element_type=F32,
    )
    mix_high = mix.astype(BF16)
    mix_low = (mix - mix_high.astype(F32)).astype(BF16)
    mix_both = jnp.concatenate([mix_high, mix_low], axis=1)

    ens_copy.wait()
    half = iota((n_member * lev, width), 1) < wide

    @pl.loop(0, coarse)
    def _(c):
        for m in range(members // 2):
            one, two = ens[2 * m, c].astype(F32), ens[2 * m + 1, c].astype(F32)
            pairs[0, m, c] = jnp.where(half, one, turned(two)).astype(BF16)
            pairs[1, m, c] = jnp.where(half, turned(one), two).astype(BF16)

    others = pl.ds(0, n_member - 1)
    most = pl.ds(0, n_space - 1)
    next_member = lax.rem(group + 1, n_member)
    next_space = lax.rem(me + 1, n_space)
    part_rows = coarse_rows // parts

    def flat(messages):
        return messages.astype(F32).reshape(slots, width).astype(BF16)

    for h in range(2):
        space_copy(send.at[h, most], recv.at[h, most], next_space, 1 + h).wait_recv()
        restricted = dot(collect[...], flat(recv[h])).astype(BF16)
        for q in range(parts):
            levels_buf[h, q, group] = restricted[q * part_rows : (q + 1) * part_rows]

            def send_levels(k, carry):
                own = levels_buf.at[h, q, group]
                member_copy(own, own, member_at(k), 3 + h * parts + q).start()
                return carry

            lax.fori_loop(0, n_member - 1, send_levels, 0)

    @pl.loop(0, fine_count, unroll=4)
    def _(b):
        interp[b] = interp[b].T

    widen_col = one_hot(iota((fine_rows, fine_count), 0) // near == iota((fine_rows, fine_count), 1))
    slot_wide = jnp.broadcast_to(slot_col, (fine_count, 128)).astype(BF16)
    place_col = dot(widen_col, slot_wide) * near + (iota((fine_rows, 128), 0) % near).astype(F32)
    for t in range(slots // 128):
        unplace[:, t * 128 : (t + 1) * 128] = one_hot(
            place_col == (iota((fine_rows, 128), 1) + t * 128).astype(F32)
        )


    for h in range(2):
        for q in range(parts):
            theirs = levels_buf.at[h, q, others]
            member_copy(theirs, theirs, next_member, 3 + h * parts + q).wait_recv()

            def coarse_four(i, carry):
                at = pl.ds(pl.multiple_of(i * 4 * near, 4 * near), 4 * near)
                slabs = [levels_buf[h, q, g, at, :].astype(F32) for g in range(n_member)]
                other = [turned(slab) for slab in slabs]
                near_half = [jnp.where(low, x, y) for x, y in zip(slabs, other)]
                far_half = [jnp.where(low, y, x) for x, y in zip(slabs, other)]
                totals = []
                for e in range(4):
                    c = q * (coarse // parts) + i * 4 + e
                    cut = slice(e * near, (e + 1) * near)
                    here = jnp.concatenate(
                        [x[cut] for both in zip(near_half, far_half) for x in both], axis=0
                    ).astype(BF16)
                    schur = jnp.concatenate(
                        [pairs[h, m, c] * here for m in range(members // 2)], axis=1
                    )
                    rebuilt = dot(mix_both, jnp.concatenate([schur, schur], axis=0))
                    total = jnp.zeros(here.shape, F32)
                    for m in range(members // 2):
                        part = rebuilt[:, m * width : (m + 1) * width]
                        total += pairs[h, m, c].astype(F32) * part
                    totals.append(total + turned(total))
                for g in range(n_member):
                    top = [t[g * lev : g * lev + near] for t in totals]
                    end = [t[g * lev + near : (g + 1) * lev] for t in totals]
                    contrib[h, q, g, at, :] = jnp.where(
                        low, jnp.concatenate(top, axis=0), jnp.concatenate(end, axis=0)
                    ).astype(BF16)
                return carry

            lax.fori_loop(0, coarse // parts // 4, coarse_four, 0)

            def send_contrib(k, carry):
                d = member_at(k)
                member_copy(
                    contrib.at[h, q, d], arrived.at[h, q, group], d, 3 + (2 + h) * parts + q
                ).start()
                return carry

            lax.fori_loop(0, n_member - 1, send_contrib, 0)
            arrived[h, q, group] = contrib[h, q, group]

    for h in range(2):
        summed = []
        for q in range(parts):
            member_copy(
                contrib.at[h, q, others],
                arrived.at[h, q, others],
                next_member,
                3 + (2 + h) * parts + q,
            ).wait_recv()
            total = arrived[h, q, 0].astype(F32)
            for g in range(1, n_member):
                total += arrived[h, q, g].astype(F32)
            summed.append((total / scale).astype(BF16))
        applied = jnp.concatenate(summed, axis=0)

        def answer(k, carry):
            at = pl.multiple_of(k * step_rows, step_rows)
            values = dot(spread[pl.ds(at, step_rows), :], applied)
            for q in range(per_step):
                p = k * per_step + q
                reply[h, p] = values[q * rows : (q + 1) * rows, :].astype(BF16)

                @pl.when(p != last)
                def _():
                    d, there = peer_at(p)
                    space_copy(
                        reply.at[h, p], back.at[h, there], d, 3 + 4 * parts + h
                    ).start()

            return carry

        lax.fori_loop(0, n_space // per_step, answer, 0)
        back[h, last] = reply[h, last]

    for h in range(2):
        space_copy(
            reply.at[h, most], back.at[h, most], next_space, 3 + 4 * parts + h
        ).wait_recv()
        fine[h] = dot(unplace[...], flat(back[h]))
    first, second = fine[0], fine[1]
    left = iota((fine_rows, width), 1) < wide
    fine[0] = jnp.where(left, first, turned(second))
    fine[1] = jnp.where(left, turned(first), second)

    @pl.loop(0, fine_count // 2, unroll=4)
    def _(i):
        at = pl.ds(pl.multiple_of(i * 2 * near, 2 * near), 2 * near)
        top, end = fine[0, at, :], fine[1, at, :]
        for e in range(2):
            cut = slice(e * near, (e + 1) * near)
            values = jnp.concatenate([top[cut], end[cut]], axis=0).astype(BF16)
            out_ref[i * 2 + e] = dot(values, interp[i * 2 + e])

    def sent(src, d, make, phase):
        make(src, src, d, phase).wait_send()

    sent(idx_send.at[most], next_space, space_copy, 0)
    for h in range(2):
        sent(send.at[h, most], next_space, space_copy, 1 + h)
        for q in range(parts):
            sent(levels_buf.at[h, q, others], next_member, member_copy, 3 + h * parts + q)
            sent(contrib.at[h, q, others], next_member, member_copy, 3 + (2 + h) * parts + q)
        sent(reply.at[h, most], next_space, space_copy, 3 + 4 * parts + h)


def on_device(increment, interp, owner, local_block, ensemble, modes):
    fine_count, lev, width = increment.shape
    members, coarse, all_lev, _ = ensemble.shape
    n_space, n_member = lax.axis_size("space"), lax.axis_size("member")
    chunks = 6
    scale = float(members * n_member - 1)
    parts, n_y = 1, 4
    dims = (
        n_space, n_member, fine_count, lev, members, coarse, width, chunks, parts, n_y, scale
    )
    near = lev // 2
    rows = CAP * near
    slots = n_space * rows
    arguments = (
        interp,
        increment,
        ensemble,
        owner.reshape(1, fine_count),
        local_block.reshape(1, fine_count),
        modes.T,
    )
    hbm = pl.BlockSpec(memory_space=pltpu.HBM)
    vmem = pl.BlockSpec(memory_space=pltpu.VMEM)
    exchange = pltpu.VMEM((2, n_space, rows, width), BF16)
    by_group = pltpu.VMEM((2, parts, n_member, coarse // parts * near, width), BF16)
    return pl.pallas_call(
        functools.partial(kernel, dims),
        out_shape=jax.ShapeDtypeStruct((fine_count, lev, width), F32),
        in_specs=[hbm] * 6,
        out_specs=vmem,
        scratch_shapes=[
            pltpu.VMEM((1, fine_count), jnp.int32),
            pltpu.VMEM((1, fine_count), jnp.int32),
            pltpu.VMEM(modes.shape[::-1], F32),
            pltpu.VMEM(interp.shape, BF16),
            pltpu.VMEM(increment.shape, BF16),
            pltpu.VMEM(ensemble.shape, BF16),
            pltpu.VMEM((2, members // 2, *ensemble.shape[1:]), BF16),
            pltpu.VMEM((2, fine_count * near, width), BF16),
            exchange,
            exchange,
            pltpu.VMEM((n_space, 1, 128), F32),
            pltpu.VMEM((n_space, 1, 128), F32),
            pltpu.VMEM((slots, fine_count * near), BF16),
            pltpu.VMEM((fine_count * near, slots), BF16),
            pltpu.VMEM((coarse * near, slots), BF16),
            pltpu.VMEM((slots, coarse * near), BF16),
            by_group,
            by_group,
            by_group,
            exchange,
            exchange,
            pltpu.VMEM((2, fine_count * near, width), F32),
            pltpu.SemaphoreType.DMA((chunks + 5,)),
            pltpu.SemaphoreType.DMA((5 + 4 * parts,)),
            pltpu.SemaphoreType.DMA((5 + 4 * parts,)),
        ],
        compiler_params=pltpu.CompilerParams(
            collective_id=0, has_side_effects=True, vmem_limit_bytes=48 * 1024 * 1024
        ),
        name="covariance_apply",
    )(*[pltpu.with_memory_space_constraint(a, pltpu.HBM) for a in arguments])


def solution(mesh):
    in_specs = (
        P("space", "member", None),
        P("space", None, None),
        P("space", None),
        P("space"),
        P("member", "space", None, None),
        P(),
    )
    out_specs = P("space", "member", None)
    return jax.shard_map(
        on_device, mesh=mesh, in_specs=in_specs, out_specs=out_specs, check_vma=False
    )
```

```python
import functools
import jax
import jax.numpy as jnp
from jax import lax
from jax.experimental import pallas as pl
from jax.experimental.pallas import tpu as pltpu
from jax.sharding import PartitionSpec as P

MESH = pl.DeviceIdType.MESH
CAP = 6
F32 = jnp.float32
BF16 = jnp.bfloat16


def iota(shape, dim):
    return lax.broadcasted_iota(jnp.int32, shape, dim)


def dot(a, b):
    return jnp.dot(a, b, preferred_element_type=F32)


def one_hot(condition):
    return jnp.where(condition, 1.0, 0.0).astype(BF16)


def kernel(
    dims,
    interp_hbm,
    inc_hbm,
    ens_hbm,
    owner_hbm,
    local_hbm,
    modes_hbm,
    out_ref,
    owner_ref,
    local_ref,
    modes_ref,
    interp,
    inc,
    ens,
    pairs,
    pieces,
    send,
    recv,
    idx_send,
    idx_recv,
    placing,
    unplace,
    collect,
    spread,
    levels_buf,
    contrib,
    arrived,
    reply,
    back,
    fine,
    load_sem,
    send_sem,
    recv_sem,
):
    n_space, n_member, fine_count, lev, members, coarse, width, chunks, parts, n_y, scale = dims
    near = lev // 2
    wide = width // 2
    rows = CAP * near
    slots = n_space * rows
    fine_rows = fine_count * near
    coarse_rows = coarse * near
    me = lax.axis_index("space")
    group = lax.axis_index("member")
    per = fine_count // chunks

    barrier = pltpu.get_barrier_semaphore()

    def greet_space(k, carry):
        peer = {"space": lax.rem(me + k, n_space)}
        pl.semaphore_signal(barrier, inc=1, device_id=peer, device_id_type=MESH)
        return carry

    def greet_member(k, carry):
        peer = {"member": lax.rem(group + k, n_member)}
        pl.semaphore_signal(barrier, inc=1, device_id=peer, device_id_type=MESH)
        return carry

    lax.fori_loop(1, n_space, greet_space, 0)
    lax.fori_loop(1, n_member, greet_member, 0)

    def load(src, dst, i):
        copy = pltpu.make_async_copy(src, dst, load_sem.at[i])
        copy.start()
        return copy

    owner_copy = load(owner_hbm, owner_ref, chunks + 2)
    local_copy = load(local_hbm, local_ref, chunks + 3)
    inc_copy = load(inc_hbm, inc, chunks)
    loads = []
    for t in range(chunks):
        part = pl.ds(t * per, per)
        loads.append(load(interp_hbm.at[part], interp.at[part], t))
    modes_copy = load(modes_hbm, modes_ref, chunks + 4)

    def member_at(k):
        third = lax.rem(k, 3)
        step = jnp.where(third == 0, 2, jnp.where(third == 1, 1, 3))
        step = jnp.where(k == n_member - 2, 0, step)
        core = lax.rem(group, 2)
        flip = (k < 3) | (k == n_member - 2)
        return lax.rem(group // 2 + step, n_member // 2) * 2 + jnp.where(flip, 1 - core, core)

    last = n_space - 1
    n_z = n_space // n_y
    my_z, my_y = me // n_y, lax.rem(me, n_y)

    def peer_at(p):
        k = last - p
        k_y, k_z = k // n_z, lax.rem(k, n_z)
        half = (k_z + 1) // 2
        up = lax.rem(k_z, 2) == 1
        step_z = jnp.where(up, half, n_z - half)
        device = lax.rem(my_z + step_z, n_z) * n_y + lax.rem(my_y + k_y, n_y)
        paired = (k_z == 0) | (k_z == n_z - 1)
        back_z = jnp.where(paired, k_z, jnp.where(up, k_z + 1, k_z - 1))
        return device, last - (lax.rem(n_y - k_y, n_y) * n_z + back_z)

    def position_of(device):
        step_z = (device // n_y - my_z + n_z) % n_z
        step_y = (device % n_y - my_y + n_y) % n_y
        k_z = jnp.where(
            step_z <= n_z // 2, jnp.maximum(2 * step_z - 1, 0), 2 * (n_z - step_z)
        )
        return last - (step_y * n_z + k_z)

    owner_copy.wait()
    local_copy.wait()
    owner_row = position_of(owner_ref[...]).astype(F32)
    down, across = iota((fine_count, fine_count), 0), iota((fine_count, fine_count), 1)
    owner_col = jnp.sum(jnp.where(down == across, owner_row, 0.0), axis=1, keepdims=True)
    same = owner_col == owner_row
    rank_row = jnp.sum(jnp.where(same & (down < across), 1.0, 0.0), axis=0, keepdims=True)
    rank_col = jnp.sum(jnp.where(same & (across < down), 1.0, 0.0), axis=1, keepdims=True)
    slot_row = owner_row * CAP + rank_row
    slot_col = owner_col * CAP + rank_col

    local_row = local_ref[...].astype(F32) + 1.0
    by_owner = jnp.where(
        iota((n_space, fine_count), 0).astype(F32) == owner_row, local_row, 0.0
    ).astype(BF16)
    by_rank = one_hot(iota((fine_count, 128), 1).astype(F32) == rank_col)
    table = dot(by_owner, by_rank)
    for d in range(n_space):
        idx_send[d] = table[d : d + 1, :]

    widen = one_hot(iota((fine_count, fine_rows), 1) // near == iota((fine_count, fine_rows), 0))
    place_row = dot(jnp.broadcast_to(slot_row, (8, fine_count)).astype(BF16), widen)[0:1]
    place_row = place_row * near + (iota((1, fine_rows), 1) % near).astype(F32)

    per_step = 8
    step_rows = per_step * rows
    for k in range(n_space // per_step):
        row = (iota((step_rows, fine_rows), 0) + k * step_rows).astype(F32)
        placing[k * step_rows : (k + 1) * step_rows, :] = one_hot(row == place_row)

    low = iota((4 * near, width), 1) < wide

    def turned(x):
        return pltpu.roll(x, wide, 1)

    inc_copy.wait()
    for t in range(chunks):
        loads[t].wait()

        @pl.loop(0, per // 4, unroll=2)
        def _(i):
            b = t * per + i * 4
            four = [dot(inc[b + q], interp[b + q]) for q in range(4)]
            first = jnp.concatenate([v[:near] for v in four], axis=0)
            second = jnp.concatenate([v[near:] for v in four], axis=0)
            at = pl.ds(pl.multiple_of(b * near, 4 * near), 4 * near)
            pieces[0, at, :] = jnp.where(low, first, turned(second)).astype(BF16)
            pieces[1, at, :] = jnp.where(low, turned(first), second).astype(BF16)

    ens_copy = load(ens_hbm, ens, chunks + 1)
    pl.semaphore_wait(barrier, n_space - 1 + n_member - 1)

    def space_copy(src, dst, d, phase):
        return pltpu.make_async_remote_copy(
            src_ref=src,
            dst_ref=dst,
            send_sem=send_sem.at[phase],
            recv_sem=recv_sem.at[phase],
            device_id={"space": d},
            device_id_type=MESH,
        )

    def member_copy(src, dst, d, phase):
        return pltpu.make_async_remote_copy(
            src_ref=src,
            dst_ref=dst,
            send_sem=send_sem.at[phase],
            recv_sem=recv_sem.at[phase],
            device_id={"member": d},
            device_id_type=MESH,
        )

    def send_idx(k, carry):
        d, there = peer_at(k)
        space_copy(idx_send.at[k], idx_recv.at[there], d, 0).start()
        return carry

    lax.fori_loop(0, last, send_idx, 0)

    for h in range(2):
        packed = pieces[h]

        def place(k, carry):
            at = pl.multiple_of(k * step_rows, step_rows)
            values = dot(placing[pl.ds(at, step_rows), :], packed)
            for q in range(per_step):
                p = k * per_step + q
                send[h, p] = values[q * rows : (q + 1) * rows, :].astype(BF16)

                @pl.when(p != last)
                def _():
                    d, there = peer_at(p)
                    space_copy(send.at[h, p], recv.at[h, there], d, 1 + h).start()

            return carry

        lax.fori_loop(0, n_space // per_step, place, 0)
        recv[h, last] = send[h, last]
    idx_recv[last] = idx_send[last]

    idx_all = space_copy(
        idx_send.at[pl.ds(0, n_space - 1)],
        idx_recv.at[pl.ds(0, n_space - 1)],
        lax.rem(me + 1, n_space),
        0,
    )
    idx_all.wait_recv()
    index = jnp.concatenate([idx_recv[s] for s in range(n_space)], axis=0).astype(BF16)
    lane_rank = one_hot((iota((128, slots), 1) % rows) // near == iota((128, slots), 0))
    by_source = dot(index, lane_rank)
    mine = iota((n_space, slots), 1) // rows == iota((n_space, slots), 0)
    index_row = jnp.sum(jnp.where(mine, by_source, 0.0), axis=0, keepdims=True)
    index_row = (index_row - 1.0) * near + (iota((1, slots), 1) % near).astype(F32)
    collect[...] = one_hot(iota((coarse_rows, slots), 0).astype(F32) == index_row)
    source_of = one_hot(iota((slots, n_space), 0) // rows == iota((slots, n_space), 1))
    by_row = dot(source_of, index)
    rank_of = (iota((slots, 128), 0) % rows) // near == iota((slots, 128), 1)
    index_col = jnp.sum(jnp.where(rank_of, by_row, 0.0), axis=1, keepdims=True)
    index_col = (index_col - 1.0) * near + (iota((slots, 1), 0) % near).astype(F32)
    spread[...] = one_hot(iota((slots, coarse_rows), 1).astype(F32) == index_col)

    modes_copy.wait()
    mix = lax.dot_general(
        modes_ref[...],
        modes_ref[...],
        (((0,), (0,)), ((), ())),
        precision=lax.Precision.HIGHEST,
        preferred_element_type=F32,
    )
    mix_high = mix.astype(BF16)
    mix_low = (mix - mix_high.astype(F32)).astype(BF16)
    mix_both = jnp.concatenate([mix_high, mix_low], axis=1)

    half = iota((n_member * lev, width), 1) < wide

    def pair_members(h):
        @pl.loop(0, coarse)
        def _(c):
            for m in range(members // 2):
                one, two = ens[2 * m, c], ens[2 * m + 1, c]
                if h == 0:
                    two = turned(two)
                else:
                    one = turned(one)
                pairs[h, m, c] = jnp.where(half, one, two)

    ens_copy.wait()
    pair_members(0)
    others = pl.ds(0, n_member - 1)
    most = pl.ds(0, n_space - 1)
    next_member = lax.rem(group + 1, n_member)
    next_space = lax.rem(me + 1, n_space)
    part_rows = coarse_rows // parts

    def flat(messages):
        return messages.astype(F32).reshape(slots, width).astype(BF16)

    for h in range(2):
        space_copy(send.at[h, most], recv.at[h, most], next_space, 1 + h).wait_recv()
        restricted = dot(collect[...], flat(recv[h])).astype(BF16)
        for q in range(parts):
            levels_buf[h, q, group] = restricted[q * part_rows : (q + 1) * part_rows]

            def send_levels(k, carry):
                own = levels_buf.at[h, q, group]
                member_copy(own, own, member_at(k), 3 + h * parts + q).start()
                return carry

            lax.fori_loop(0, n_member - 1, send_levels, 0)

        if h == 0:
            pair_members(1)

    for h in range(2):
        for q in range(parts):
            theirs = levels_buf.at[h, q, others]
            member_copy(theirs, theirs, next_member, 3 + h * parts + q).wait_recv()

            def coarse_four(i, carry):
                at = pl.ds(pl.multiple_of(i * 4 * near, 4 * near), 4 * near)
                slabs = [levels_buf[h, q, g, at, :].astype(F32) for g in range(n_member)]
                other = [turned(slab) for slab in slabs]
                near_half = [jnp.where(low, x, y) for x, y in zip(slabs, other)]
                far_half = [jnp.where(low, y, x) for x, y in zip(slabs, other)]
                totals = []
                for e in range(4):
                    c = q * (coarse // parts) + i * 4 + e
                    cut = slice(e * near, (e + 1) * near)
                    here = jnp.concatenate(
                        [x[cut] for both in zip(near_half, far_half) for x in both], axis=0
                    ).astype(BF16)
                    schur = jnp.concatenate(
                        [pairs[h, m, c] * here for m in range(members // 2)], axis=1
                    )
                    rebuilt = dot(mix_both, jnp.concatenate([schur, schur], axis=0))
                    total = jnp.zeros(here.shape, F32)
                    for m in range(members // 2):
                        part = rebuilt[:, m * width : (m + 1) * width]
                        total += pairs[h, m, c].astype(F32) * part
                    totals.append(total + turned(total))
                for g in range(n_member):
                    top = [t[g * lev : g * lev + near] for t in totals]
                    end = [t[g * lev + near : (g + 1) * lev] for t in totals]
                    contrib[h, q, g, at, :] = jnp.where(
                        low, jnp.concatenate(top, axis=0), jnp.concatenate(end, axis=0)
                    ).astype(BF16)
                return carry

            lax.fori_loop(0, coarse // parts // 4, coarse_four, 0)

            def send_contrib(k, carry):
                d = member_at(k)
                member_copy(
                    contrib.at[h, q, d], arrived.at[h, q, group], d, 3 + (2 + h) * parts + q
                ).start()
                return carry

            lax.fori_loop(0, n_member - 1, send_contrib, 0)
            arrived[h, q, group] = contrib[h, q, group]

    for h in range(2):
        summed = []
        for q in range(parts):
            member_copy(
                contrib.at[h, q, others],
                arrived.at[h, q, others],
                next_member,
                3 + (2 + h) * parts + q,
            ).wait_recv()
            total = arrived[h, q, 0].astype(F32)
            for g in range(1, n_member):
                total += arrived[h, q, g].astype(F32)
            summed.append((total / scale).astype(BF16))
        applied = jnp.concatenate(summed, axis=0)

        def answer(k, carry):
            at = pl.multiple_of(k * step_rows, step_rows)
            values = dot(spread[pl.ds(at, step_rows), :], applied)
            for q in range(per_step):
                p = k * per_step + q
                reply[h, p] = values[q * rows : (q + 1) * rows, :].astype(BF16)

                @pl.when(p != last)
                def _():
                    d, there = peer_at(p)
                    space_copy(
                        reply.at[h, p], back.at[h, there], d, 3 + 4 * parts + h
                    ).start()

            return carry

        lax.fori_loop(0, n_space // per_step, answer, 0)
        back[h, last] = reply[h, last]

    @pl.loop(0, fine_count, unroll=4)
    def _(b):
        interp[b] = interp[b].T

    widen_col = one_hot(iota((fine_rows, fine_count), 0) // near == iota((fine_rows, fine_count), 1))
    slot_wide = jnp.broadcast_to(slot_col, (fine_count, 128)).astype(BF16)
    place_col = dot(widen_col, slot_wide) * near + (iota((fine_rows, 128), 0) % near).astype(F32)
    for t in range(slots // 128):
        unplace[:, t * 128 : (t + 1) * 128] = one_hot(
            place_col == (iota((fine_rows, 128), 1) + t * 128).astype(F32)
        )


    for h in range(2):
        space_copy(
            reply.at[h, most], back.at[h, most], next_space, 3 + 4 * parts + h
        ).wait_recv()
        fine[h] = dot(unplace[...], flat(back[h]))
    first, second = fine[0], fine[1]
    left = iota((fine_rows, width), 1) < wide
    fine[0] = jnp.where(left, first, turned(second))
    fine[1] = jnp.where(left, turned(first), second)

    @pl.loop(0, fine_count // 2, unroll=4)
    def _(i):
        at = pl.ds(pl.multiple_of(i * 2 * near, 2 * near), 2 * near)
        top, end = fine[0, at, :], fine[1, at, :]
        for e in range(2):
            cut = slice(e * near, (e + 1) * near)
            values = jnp.concatenate([top[cut], end[cut]], axis=0).astype(BF16)
            out_ref[i * 2 + e] = dot(values, interp[i * 2 + e])

    def sent(src, d, make, phase):
        make(src, src, d, phase).wait_send()

    sent(idx_send.at[most], next_space, space_copy, 0)
    for h in range(2):
        sent(send.at[h, most], next_space, space_copy, 1 + h)
        for q in range(parts):
            sent(levels_buf.at[h, q, others], next_member, member_copy, 3 + h * parts + q)
            sent(contrib.at[h, q, others], next_member, member_copy, 3 + (2 + h) * parts + q)
        sent(reply.at[h, most], next_space, space_copy, 3 + 4 * parts + h)


def on_device(increment, interp, owner, local_block, ensemble, modes):
    fine_count, lev, width = increment.shape
    members, coarse, all_lev, _ = ensemble.shape
    n_space, n_member = lax.axis_size("space"), lax.axis_size("member")
    chunks = 6
    scale = float(members * n_member - 1)
    parts, n_y = 1, 4
    dims = (
        n_space, n_member, fine_count, lev, members, coarse, width, chunks, parts, n_y, scale
    )
    near = lev // 2
    rows = CAP * near
    slots = n_space * rows
    arguments = (
        interp,
        increment,
        ensemble,
        owner.reshape(1, fine_count),
        local_block.reshape(1, fine_count),
        modes.T,
    )
    hbm = pl.BlockSpec(memory_space=pltpu.HBM)
    vmem = pl.BlockSpec(memory_space=pltpu.VMEM)
    exchange = pltpu.VMEM((2, n_space, rows, width), BF16)
    by_group = pltpu.VMEM((2, parts, n_member, coarse // parts * near, width), BF16)
    return pl.pallas_call(
        functools.partial(kernel, dims),
        out_shape=jax.ShapeDtypeStruct((fine_count, lev, width), F32),
        in_specs=[hbm] * 6,
        out_specs=vmem,
        scratch_shapes=[
            pltpu.VMEM((1, fine_count), jnp.int32),
            pltpu.VMEM((1, fine_count), jnp.int32),
            pltpu.VMEM(modes.shape[::-1], F32),
            pltpu.VMEM(interp.shape, BF16),
            pltpu.VMEM(increment.shape, BF16),
            pltpu.VMEM(ensemble.shape, BF16),
            pltpu.VMEM((2, members // 2, *ensemble.shape[1:]), BF16),
            pltpu.VMEM((2, fine_count * near, width), BF16),
            exchange,
            exchange,
            pltpu.VMEM((n_space, 1, 128), F32),
            pltpu.VMEM((n_space, 1, 128), F32),
            pltpu.VMEM((slots, fine_count * near), BF16),
            pltpu.VMEM((fine_count * near, slots), BF16),
            pltpu.VMEM((coarse * near, slots), BF16),
            pltpu.VMEM((slots, coarse * near), BF16),
            by_group,
            by_group,
            by_group,
            exchange,
            exchange,
            pltpu.VMEM((2, fine_count * near, width), F32),
            pltpu.SemaphoreType.DMA((chunks + 5,)),
            pltpu.SemaphoreType.DMA((5 + 4 * parts,)),
            pltpu.SemaphoreType.DMA((5 + 4 * parts,)),
        ],
        compiler_params=pltpu.CompilerParams(
            collective_id=0, has_side_effects=True, vmem_limit_bytes=48 * 1024 * 1024
        ),
        name="covariance_apply",
    )(*[pltpu.with_memory_space_constraint(a, pltpu.HBM) for a in arguments])


def solution(mesh):
    in_specs = (
        P("space", "member", None),
        P("space", None, None),
        P("space", None),
        P("space"),
        P("member", "space", None, None),
        P(),
    )
    out_specs = P("space", "member", None)
    return jax.shard_map(
        on_device, mesh=mesh, in_specs=in_specs, out_specs=out_specs, check_vma=False
    )
```

```python
import functools
import jax
import jax.numpy as jnp
from jax import lax
from jax.experimental import pallas as pl
from jax.experimental.pallas import tpu as pltpu
from jax.sharding import PartitionSpec as P

MESH = pl.DeviceIdType.MESH
CAP = 6
F32 = jnp.float32
BF16 = jnp.bfloat16


def iota(shape, dim):
    return lax.broadcasted_iota(jnp.int32, shape, dim)


def dot(a, b):
    return jnp.dot(a, b, preferred_element_type=F32)


def one_hot(condition):
    return jnp.where(condition, 1.0, 0.0).astype(BF16)


def kernel(
    dims,
    interp_hbm,
    inc_hbm,
    ens_hbm,
    owner_hbm,
    local_hbm,
    modes_hbm,
    out_ref,
    owner_ref,
    local_ref,
    modes_ref,
    interp,
    inc,
    ens,
    pairs,
    pieces,
    send,
    recv,
    idx_send,
    idx_recv,
    placing,
    unplace,
    collect,
    spread,
    levels_buf,
    contrib,
    arrived,
    reply,
    back,
    fine,
    load_sem,
    send_sem,
    recv_sem,
):
    n_space, n_member, fine_count, lev, members, coarse, width, chunks, parts, n_y, scale = dims
    near = lev // 2
    wide = width // 2
    rows = CAP * near
    slots = n_space * rows
    fine_rows = fine_count * near
    coarse_rows = coarse * near
    me = lax.axis_index("space")
    group = lax.axis_index("member")
    per = fine_count // chunks

    barrier = pltpu.get_barrier_semaphore()

    def greet_space(k, carry):
        peer = {"space": lax.rem(me + k, n_space)}
        pl.semaphore_signal(barrier, inc=1, device_id=peer, device_id_type=MESH)
        return carry

    def greet_member(k, carry):
        peer = {"member": lax.rem(group + k, n_member)}
        pl.semaphore_signal(barrier, inc=1, device_id=peer, device_id_type=MESH)
        return carry

    lax.fori_loop(1, n_space, greet_space, 0)
    lax.fori_loop(1, n_member, greet_member, 0)

    def load(src, dst, i):
        copy = pltpu.make_async_copy(src, dst, load_sem.at[i])
        copy.start()
        return copy

    owner_copy = load(owner_hbm, owner_ref, chunks + 2)
    local_copy = load(local_hbm, local_ref, chunks + 3)
    inc_copy = load(inc_hbm, inc, chunks)
    loads = []
    for t in range(chunks):
        part = pl.ds(t * per, per)
        loads.append(load(interp_hbm.at[part], interp.at[part], t))
    modes_copy = load(modes_hbm, modes_ref, chunks + 4)

    def member_at(k):
        third = lax.rem(k, 3)
        step = jnp.where(third == 0, 2, jnp.where(third == 1, 1, 3))
        step = jnp.where(k == n_member - 2, 0, step)
        core = lax.rem(group, 2)
        flip = (k < 3) | (k == n_member - 2)
        return lax.rem(group // 2 + step, n_member // 2) * 2 + jnp.where(flip, 1 - core, core)

    last = n_space - 1
    n_z = n_space // n_y
    my_z, my_y = me // n_y, lax.rem(me, n_y)

    def peer_at(p):
        k = last - p
        k_y, k_z = k // n_z, lax.rem(k, n_z)
        half = (k_z + 1) // 2
        up = lax.rem(k_z, 2) == 1
        step_z = jnp.where(up, half, n_z - half)
        device = lax.rem(my_z + step_z, n_z) * n_y + lax.rem(my_y + k_y, n_y)
        paired = (k_z == 0) | (k_z == n_z - 1)
        back_z = jnp.where(paired, k_z, jnp.where(up, k_z + 1, k_z - 1))
        return device, last - (lax.rem(n_y - k_y, n_y) * n_z + back_z)

    def position_of(device):
        step_z = (device // n_y - my_z + n_z) % n_z
        step_y = (device % n_y - my_y + n_y) % n_y
        k_z = jnp.where(
            step_z <= n_z // 2, jnp.maximum(2 * step_z - 1, 0), 2 * (n_z - step_z)
        )
        return last - (step_y * n_z + k_z)

    owner_copy.wait()
    local_copy.wait()
    owner_row = position_of(owner_ref[...]).astype(F32)
    down, across = iota((fine_count, fine_count), 0), iota((fine_count, fine_count), 1)
    owner_col = jnp.sum(jnp.where(down == across, owner_row, 0.0), axis=1, keepdims=True)
    same = owner_col == owner_row
    rank_row = jnp.sum(jnp.where(same & (down < across), 1.0, 0.0), axis=0, keepdims=True)
    rank_col = jnp.sum(jnp.where(same & (across < down), 1.0, 0.0), axis=1, keepdims=True)
    slot_row = owner_row * CAP + rank_row
    slot_col = owner_col * CAP + rank_col

    local_row = local_ref[...].astype(F32) + 1.0
    by_owner = jnp.where(
        iota((n_space, fine_count), 0).astype(F32) == owner_row, local_row, 0.0
    ).astype(BF16)
    by_rank = one_hot(iota((fine_count, 128), 1).astype(F32) == rank_col)
    table = dot(by_owner, by_rank)
    for d in range(n_space):
        idx_send[d] = table[d : d + 1, :]

    widen = one_hot(iota((fine_count, fine_rows), 1) // near == iota((fine_count, fine_rows), 0))
    place_row = dot(jnp.broadcast_to(slot_row, (8, fine_count)).astype(BF16), widen)[0:1]
    place_row = place_row * near + (iota((1, fine_rows), 1) % near).astype(F32)

    per_step = 8
    step_rows = per_step * rows
    for k in range(n_space // per_step):
        row = (iota((step_rows, fine_rows), 0) + k * step_rows).astype(F32)
        placing[k * step_rows : (k + 1) * step_rows, :] = one_hot(row == place_row)

    low = iota((4 * near, width), 1) < wide

    def turned(x):
        return pltpu.roll(x, wide, 1)

    inc_copy.wait()
    for t in range(chunks):
        loads[t].wait()

        @pl.loop(0, per // 4, unroll=4)
        def _(i):
            b = t * per + i * 4
            four = [dot(inc[b + q], interp[b + q]) for q in range(4)]
            first = jnp.concatenate([v[:near] for v in four], axis=0)
            second = jnp.concatenate([v[near:] for v in four], axis=0)
            at = pl.ds(pl.multiple_of(b * near, 4 * near), 4 * near)
            pieces[0, at, :] = jnp.where(low, first, turned(second)).astype(BF16)
            pieces[1, at, :] = jnp.where(low, turned(first), second).astype(BF16)

    ens_copy = load(ens_hbm, ens, chunks + 1)
    pl.semaphore_wait(barrier, n_space - 1 + n_member - 1)

    def space_copy(src, dst, d, phase):
        return pltpu.make_async_remote_copy(
            src_ref=src,
            dst_ref=dst,
            send_sem=send_sem.at[phase],
            recv_sem=recv_sem.at[phase],
            device_id={"space": d},
            device_id_type=MESH,
        )

    def member_copy(src, dst, d, phase):
        return pltpu.make_async_remote_copy(
            src_ref=src,
            dst_ref=dst,
            send_sem=send_sem.at[phase],
            recv_sem=recv_sem.at[phase],
            device_id={"member": d},
            device_id_type=MESH,
        )

    def send_idx(k, carry):
        d, there = peer_at(k)
        space_copy(idx_send.at[k], idx_recv.at[there], d, 0).start()
        return carry

    lax.fori_loop(0, last, send_idx, 0)

    for h in range(2):
        packed = pieces[h]

        def place(k, carry):
            at = pl.multiple_of(k * step_rows, step_rows)
            values = dot(placing[pl.ds(at, step_rows), :], packed)
            for q in range(per_step):
                p = k * per_step + q
                send[h, p] = values[q * rows : (q + 1) * rows, :].astype(BF16)

                @pl.when(p != last)
                def _():
                    d, there = peer_at(p)
                    space_copy(send.at[h, p], recv.at[h, there], d, 1 + h).start()

            return carry

        lax.fori_loop(0, n_space // per_step, place, 0)
        recv[h, last] = send[h, last]
    idx_recv[last] = idx_send[last]

    idx_all = space_copy(
        idx_send.at[pl.ds(0, n_space - 1)],
        idx_recv.at[pl.ds(0, n_space - 1)],
        lax.rem(me + 1, n_space),
        0,
    )
    idx_all.wait_recv()
    index = jnp.concatenate([idx_recv[s] for s in range(n_space)], axis=0).astype(BF16)
    lane_rank = one_hot((iota((128, slots), 1) % rows) // near == iota((128, slots), 0))
    by_source = dot(index, lane_rank)
    mine = iota((n_space, slots), 1) // rows == iota((n_space, slots), 0)
    index_row = jnp.sum(jnp.where(mine, by_source, 0.0), axis=0, keepdims=True)
    index_row = (index_row - 1.0) * near + (iota((1, slots), 1) % near).astype(F32)
    collect[...] = one_hot(iota((coarse_rows, slots), 0).astype(F32) == index_row)
    modes_copy.wait()
    mix = lax.dot_general(
        modes_ref[...],
        modes_ref[...],
        (((0,), (0,)), ((), ())),
        precision=lax.Precision.HIGHEST,
        preferred_element_type=F32,
    )
    mix_high = mix.astype(BF16)
    mix_low = (mix - mix_high.astype(F32)).astype(BF16)
    mix_both = jnp.concatenate([mix_high, mix_low], axis=1)

    half = iota((n_member * lev, width), 1) < wide

    def pair_members(h):
        @pl.loop(0, coarse, unroll=4)
        def _(c):
            for m in range(members // 2):
                one, two = ens[2 * m, c], ens[2 * m + 1, c]
                if h == 0:
                    two = turned(two)
                else:
                    one = turned(one)
                pairs[h, m, c] = jnp.where(half, one, two)

    ens_copy.wait()
    pair_members(0)
    others = pl.ds(0, n_member - 1)
    most = pl.ds(0, n_space - 1)
    next_member = lax.rem(group + 1, n_member)
    next_space = lax.rem(me + 1, n_space)
    part_rows = coarse_rows // parts

    def flat(messages):
        return messages.astype(F32).reshape(slots, width).astype(BF16)

    for h in range(2):
        space_copy(send.at[h, most], recv.at[h, most], next_space, 1 + h).wait_recv()
        restricted = dot(collect[...], flat(recv[h])).astype(BF16)
        for q in range(parts):
            levels_buf[h, q, group] = restricted[q * part_rows : (q + 1) * part_rows]

            def send_levels(k, carry):
                own = levels_buf.at[h, q, group]
                member_copy(own, own, member_at(k), 3 + h * parts + q).start()
                return carry

            lax.fori_loop(0, n_member - 1, send_levels, 0)

        if h == 0:
            pair_members(1)

    for h in range(2):
        for q in range(parts):
            theirs = levels_buf.at[h, q, others]
            member_copy(theirs, theirs, next_member, 3 + h * parts + q).wait_recv()

            def coarse_four(i, carry):
                at = pl.ds(pl.multiple_of(i * 4 * near, 4 * near), 4 * near)
                slabs = [levels_buf[h, q, g, at, :].astype(F32) for g in range(n_member)]
                other = [turned(slab) for slab in slabs]
                near_half = [jnp.where(low, x, y) for x, y in zip(slabs, other)]
                far_half = [jnp.where(low, y, x) for x, y in zip(slabs, other)]
                totals = []
                for e in range(4):
                    c = q * (coarse // parts) + i * 4 + e
                    cut = slice(e * near, (e + 1) * near)
                    here = jnp.concatenate(
                        [x[cut] for both in zip(near_half, far_half) for x in both], axis=0
                    ).astype(BF16)
                    schur = jnp.concatenate(
                        [pairs[h, m, c] * here for m in range(members // 2)], axis=1
                    )
                    rebuilt = dot(mix_both, jnp.concatenate([schur, schur], axis=0))
                    total = jnp.zeros(here.shape, F32)
                    for m in range(members // 2):
                        part = rebuilt[:, m * width : (m + 1) * width]
                        total += pairs[h, m, c].astype(F32) * part
                    totals.append(total + turned(total))
                for g in range(n_member):
                    top = [t[g * lev : g * lev + near] for t in totals]
                    end = [t[g * lev + near : (g + 1) * lev] for t in totals]
                    contrib[h, q, g, at, :] = jnp.where(
                        low, jnp.concatenate(top, axis=0), jnp.concatenate(end, axis=0)
                    ).astype(BF16)
                return carry

            lax.fori_loop(0, coarse // parts // 4, coarse_four, 0)

            def send_contrib(k, carry):
                d = member_at(k)
                member_copy(
                    contrib.at[h, q, d], arrived.at[h, q, group], d, 3 + (2 + h) * parts + q
                ).start()
                return carry

            lax.fori_loop(0, n_member - 1, send_contrib, 0)
            arrived[h, q, group] = contrib[h, q, group]

        if h == 0:
            source_of = one_hot(iota((slots, n_space), 0) // rows == iota((slots, n_space), 1))
            by_row = dot(source_of, index)
            rank_of = (iota((slots, 128), 0) % rows) // near == iota((slots, 128), 1)
            index_col = jnp.sum(jnp.where(rank_of, by_row, 0.0), axis=1, keepdims=True)
            index_col = (index_col - 1.0) * near + (iota((slots, 1), 0) % near).astype(F32)
            spread[...] = one_hot(iota((slots, coarse_rows), 1).astype(F32) == index_col)


    for h in range(2):
        summed = []
        for q in range(parts):
            member_copy(
                contrib.at[h, q, others],
                arrived.at[h, q, others],
                next_member,
                3 + (2 + h) * parts + q,
            ).wait_recv()
            total = arrived[h, q, 0].astype(F32)
            for g in range(1, n_member):
                total += arrived[h, q, g].astype(F32)
            summed.append((total / scale).astype(BF16))
        applied = jnp.concatenate(summed, axis=0)

        def answer(k, carry):
            at = pl.multiple_of(k * step_rows, step_rows)
            values = dot(spread[pl.ds(at, step_rows), :], applied)
            for q in range(per_step):
                p = k * per_step + q
                reply[h, p] = values[q * rows : (q + 1) * rows, :].astype(BF16)

                @pl.when(p != last)
                def _():
                    d, there = peer_at(p)
                    space_copy(
                        reply.at[h, p], back.at[h, there], d, 3 + 4 * parts + h
                    ).start()

            return carry

        lax.fori_loop(0, n_space // per_step, answer, 0)
        back[h, last] = reply[h, last]

    @pl.loop(0, fine_count, unroll=4)
    def _(b):
        interp[b] = interp[b].T

    widen_col = one_hot(iota((fine_rows, fine_count), 0) // near == iota((fine_rows, fine_count), 1))
    slot_wide = jnp.broadcast_to(slot_col, (fine_count, 128)).astype(BF16)
    place_col = dot(widen_col, slot_wide) * near + (iota((fine_rows, 128), 0) % near).astype(F32)
    for t in range(slots // 128):
        unplace[:, t * 128 : (t + 1) * 128] = one_hot(
            place_col == (iota((fine_rows, 128), 1) + t * 128).astype(F32)
        )


    for h in range(2):
        space_copy(
            reply.at[h, most], back.at[h, most], next_space, 3 + 4 * parts + h
        ).wait_recv()
        fine[h] = dot(unplace[...], flat(back[h]))
    first, second = fine[0], fine[1]
    left = iota((fine_rows, width), 1) < wide
    fine[0] = jnp.where(left, first, turned(second))
    fine[1] = jnp.where(left, turned(first), second)

    @pl.loop(0, fine_count // 2, unroll=12)
    def _(i):
        at = pl.ds(pl.multiple_of(i * 2 * near, 2 * near), 2 * near)
        top, end = fine[0, at, :], fine[1, at, :]
        for e in range(2):
            cut = slice(e * near, (e + 1) * near)
            values = jnp.concatenate([top[cut], end[cut]], axis=0).astype(BF16)
            out_ref[i * 2 + e] = dot(values, interp[i * 2 + e])

    def sent(src, d, make, phase):
        make(src, src, d, phase).wait_send()

    sent(idx_send.at[most], next_space, space_copy, 0)
    for h in range(2):
        sent(send.at[h, most], next_space, space_copy, 1 + h)
        for q in range(parts):
            sent(levels_buf.at[h, q, others], next_member, member_copy, 3 + h * parts + q)
            sent(contrib.at[h, q, others], next_member, member_copy, 3 + (2 + h) * parts + q)
        sent(reply.at[h, most], next_space, space_copy, 3 + 4 * parts + h)


def on_device(increment, interp, owner, local_block, ensemble, modes):
    fine_count, lev, width = increment.shape
    members, coarse, all_lev, _ = ensemble.shape
    n_space, n_member = lax.axis_size("space"), lax.axis_size("member")
    chunks = 6
    scale = float(members * n_member - 1)
    parts, n_y = 1, 4
    dims = (
        n_space, n_member, fine_count, lev, members, coarse, width, chunks, parts, n_y, scale
    )
    near = lev // 2
    rows = CAP * near
    slots = n_space * rows
    arguments = (
        interp,
        increment,
        ensemble,
        owner.reshape(1, fine_count),
        local_block.reshape(1, fine_count),
        modes.T,
    )
    hbm = pl.BlockSpec(memory_space=pltpu.HBM)
    vmem = pl.BlockSpec(memory_space=pltpu.VMEM)
    exchange = pltpu.VMEM((2, n_space, rows, width), BF16)
    by_group = pltpu.VMEM((2, parts, n_member, coarse // parts * near, width), BF16)
    return pl.pallas_call(
        functools.partial(kernel, dims),
        out_shape=jax.ShapeDtypeStruct((fine_count, lev, width), F32),
        in_specs=[hbm] * 6,
        out_specs=vmem,
        scratch_shapes=[
            pltpu.VMEM((1, fine_count), jnp.int32),
            pltpu.VMEM((1, fine_count), jnp.int32),
            pltpu.VMEM(modes.shape[::-1], F32),
            pltpu.VMEM(interp.shape, BF16),
            pltpu.VMEM(increment.shape, BF16),
            pltpu.VMEM(ensemble.shape, BF16),
            pltpu.VMEM((2, members // 2, *ensemble.shape[1:]), BF16),
            pltpu.VMEM((2, fine_count * near, width), BF16),
            exchange,
            exchange,
            pltpu.VMEM((n_space, 1, 128), F32),
            pltpu.VMEM((n_space, 1, 128), F32),
            pltpu.VMEM((slots, fine_count * near), BF16),
            pltpu.VMEM((fine_count * near, slots), BF16),
            pltpu.VMEM((coarse * near, slots), BF16),
            pltpu.VMEM((slots, coarse * near), BF16),
            by_group,
            by_group,
            by_group,
            exchange,
            exchange,
            pltpu.VMEM((2, fine_count * near, width), F32),
            pltpu.SemaphoreType.DMA((chunks + 5,)),
            pltpu.SemaphoreType.DMA((5 + 4 * parts,)),
            pltpu.SemaphoreType.DMA((5 + 4 * parts,)),
        ],
        compiler_params=pltpu.CompilerParams(
            collective_id=0, has_side_effects=True, vmem_limit_bytes=48 * 1024 * 1024
        ),
        name="covariance_apply",
    )(*[pltpu.with_memory_space_constraint(a, pltpu.HBM) for a in arguments])


def solution(mesh):
    in_specs = (
        P("space", "member", None),
        P("space", None, None),
        P("space", None),
        P("space"),
        P("member", "space", None, None),
        P(),
    )
    out_specs = P("space", "member", None)
    return jax.shard_map(
        on_device, mesh=mesh, in_specs=in_specs, out_specs=out_specs, check_vma=False
    )
```
